128 devices in a mesh: seq: 32 (over z, x, core), rep: 4 (over y).
Axes of the slice: x: 4, y: 4, z: 4, core: 2. Of those that a mesh axis runs over, the one named last changes fastest.
Arguments:
- tokens: bfloat16 [16384, 2304], P(('rep', 'seq')), parts along dimension 0, may hold values from -6 to 6
- qkv_weight: bfloat16 [2304, 6144], P(None, 'seq'), may hold values from -0.125 to 0.125
- conv_weight: float32 [4, 6144], replicated, may hold values from -3 to 3
- decay_down: bfloat16 [2304, 128], replicated, may hold values from -0.125 to 0.125
- decay_up: bfloat16 [128, 2048], replicated, may hold values from -0.5 to 0.5
- decay_rate: float32 [2048], replicated, may hold values from 0.00024414062 to 0.1
- beta_weight: bfloat16 [2304, 16], replicated, may hold values from -0.125 to 0.125
- beta_scale: float32 [16], replicated, may hold values from 0.03125 to 1
- gate_down: bfloat16 [2304, 128], replicated, may hold values from -0.125 to 0.125
- gate_up: bfloat16 [128, 2048], replicated, may hold values from -0.5 to 0.5
- norm_gain: float32 [128], replicated, may hold values from 0.1 to 1.9
Outputs:
- attended: bfloat16 [16384, 2048], P(('rep', 'seq')), parts along dimension 0
The draws below stay inside these ranges and needn't reach their ends.
There are 4 independent parts, one for each index of `rep`. The reference program is written for one: setup_inputs(seed, part) draws one part's arguments, and reference() takes and returns one part's arrays. A program takes and returns all parts, laid end to end along the dimension named above; an argument that names none is the same for every part. Nothing has to cross between parts.
All inputs are finite; a program needn't handle non-finite values.
Results may differ from the reference program's by a relative error of at most 0.0054.
Values may be sent and summed in bfloat16 or wider, within the bound.
No kernel may reach another device: no remote copies, remote signals or barrier semaphores. Data moves between devices by JAX's collectives and lax.ppermute only.
A program may use at most 192 MiB of HBM per device.

```python
import math
import jax
import jax.numpy as jnp
from jax import lax

D = 2304
H = 16
DK = 128
RANK = 128
CONV = 4
BLOCK = 64
TOKENS = 4096
HV = 2048


def draw_beta_scale(key, part):
    picker = jax.random.fold_in(key, 11)
    spread_key = jax.random.fold_in(key, 12)
    upper_key = jax.random.fold_in(key, 13)
    order = jax.random.permutation(picker, H)
    lasting = order >= H // 2
    level = jnp.exp(jax.random.uniform(spread_key, (H,), jnp.float32, 0.0, math.log(4.0)))
    quick = jax.random.uniform(upper_key, (H,), jnp.float32, 0.5, 1.0)
    return jnp.where(lasting, level * (DK / TOKENS), quick).astype(jnp.float32)


def block_levels(key, shape, split, smallest, high):
    gain = 1.0
    for position, parts in split:
        draws = jax.random.uniform(jax.random.fold_in(jax.random.fold_in(key, 6), position), (parts,), jnp.float32, smallest / len(split), high / len(split))
        gain = gain * jnp.repeat(jnp.exp(draws), shape[position] // parts).reshape((-1,) + (1,) * (len(shape) - 1 - position))
    return gain


def scatter_about(own_key, dims, deviation, most, split=(), kind=jnp.bfloat16):
    drawn = deviation * jax.random.normal(own_key, dims, jnp.float32)
    if split:
        drawn = drawn * block_levels(own_key, dims, split, -0.22, 0.18)
    return jnp.clip(drawn, -most, most).astype(kind)


def setup_inputs(seed: int = 0, part: int = 0) -> dict:
    streams_of = jax.random.split(jax.random.key(seed), 12)
    part_keys = jax.random.split(jax.random.fold_in(streams_of[11], part), 12)
    tokens = scatter_about(part_keys[0], (TOKENS, D), 1.0, 6.0, ((0, 32),))
    qkv_weight = scatter_about(streams_of[1], (D, 3 * HV), D ** -0.5, 0.125, ((1, 32),))
    conv_weight = scatter_about(streams_of[2], (CONV, 3 * HV), 0.5, 3.0, (), jnp.float32)
    decay_down = scatter_about(streams_of[3], (D, RANK), D ** -0.5, 0.125)
    decay_up = scatter_about(streams_of[4], (RANK, HV), RANK ** -0.5, 0.5)
    decay_rate = jnp.clip(jnp.exp(jax.random.uniform(streams_of[5], (HV,), jnp.float32, math.log(0.00024414062), math.log(0.1))), 0.00024414062, 0.1)
    beta_weight = scatter_about(streams_of[6], (D, H), D ** -0.5, 0.125)
    beta_scale = draw_beta_scale(jax.random.fold_in(streams_of[11], 71), part)
    gate_down = scatter_about(streams_of[8], (D, RANK), D ** -0.5, 0.125)
    gate_up = scatter_about(streams_of[9], (RANK, HV), RANK ** -0.5, 0.5)
    norm_gain = jnp.clip(1.0 + 0.18 * jax.random.normal(streams_of[10], (DK,), jnp.float32), 0.1, 1.9)
    return {"tokens": tokens, "qkv_weight": qkv_weight, "conv_weight": conv_weight, "decay_down": decay_down, "decay_up": decay_up, "decay_rate": decay_rate, "beta_weight": beta_weight, "beta_scale": beta_scale, "gate_down": gate_down, "gate_up": gate_up, "norm_gain": norm_gain}


precise = lax.Precision.HIGHEST

def unit_rows(vector):
    return vector * lax.rsqrt(lax.optimization_barrier(jnp.sum(vector * vector, axis=-1, keepdims=True)) + 1e-06)

def features(padded, count, conv_weight):
    combined = conv_weight[0] * padded[0:count].astype(jnp.float32)
    for offset in range(1, CONV):
        combined = combined + conv_weight[offset] * padded[offset:offset + count].astype(jnp.float32)
    active = jax.nn.silu(combined).reshape(count, 3, H, DK)
    query = unit_rows(active[:, 0]) * DK ** (-0.5)
    keys = unit_rows(active[:, 1])
    values = active[:, 2]
    return (query, keys, values)

def gates(tokens, decay_down, decay_up, decay_rate, beta_weight, beta_scale, gate_down, gate_up):
    beta = beta_scale * jax.nn.sigmoid(jnp.dot(tokens.astype(jnp.float32), beta_weight.astype(jnp.float32), preferred_element_type=jnp.float32))
    decay_low = jnp.dot(tokens.astype(jnp.float32), decay_down.astype(jnp.float32), preferred_element_type=jnp.float32).astype(jnp.bfloat16)
    logdec = -decay_rate * jax.nn.sigmoid(jnp.dot(decay_low.astype(jnp.float32), decay_up.astype(jnp.float32), preferred_element_type=jnp.float32))
    gate_low = jnp.dot(tokens.astype(jnp.float32), gate_down.astype(jnp.float32), preferred_element_type=jnp.float32).astype(jnp.bfloat16)
    gate_value = jax.nn.sigmoid(jnp.dot(gate_low.astype(jnp.float32), gate_up.astype(jnp.float32), preferred_element_type=jnp.float32))
    return (beta, logdec, gate_value)

def to_blocks(array, count):
    return array.reshape(count // BLOCK, BLOCK, H, array.shape[-1]).transpose(0, 2, 1, 3)

def block_terms(query, keys, values, beta, logdec):
    log_sum = jnp.cumsum(logdec, axis=2)
    grow = jnp.exp(log_sum)
    keys_up = keys * grow
    keys_down = keys * jnp.exp(-log_sum)
    query_up = query * grow
    keys_end = keys * jnp.exp(log_sum[:, :, -1:, :] - log_sum)
    length = query.shape[2]
    rows = lax.broadcasted_iota(jnp.int32, (length, length), 0)
    columns = lax.broadcasted_iota(jnp.int32, (length, length), 1)
    scores = jnp.einsum('nhic,nhjc->nhij', keys_up, keys_down, precision=precise) * beta[..., None]
    system = jnp.where(rows > columns, scores, 0.0) + jnp.eye(length, dtype=jnp.float32)
    right_side = jnp.concatenate([values, keys_up], axis=-1) * beta[..., None]
    solved = jax.scipy.linalg.solve_triangular(system, right_side, lower=True, unit_diagonal=True)
    values_w = solved[..., :DK]
    keys_w = solved[..., DK:]
    attend = jnp.where(rows >= columns, jnp.einsum('nhic,nhjc->nhij', query_up, keys_down, precision=precise), 0.0)
    decay_end = jnp.exp(log_sum[:, :, -1, :])
    return (query_up, keys_end, values_w, keys_w, attend, decay_end)

def advance(state, inputs):
    query_up, keys_end, values_w, keys_w, attend, decay_end = inputs
    update = values_w - jnp.einsum('hcd,hde->hce', keys_w, state, precision=precise)
    output = jnp.einsum('hcd,hde->hce', query_up, state, precision=precise)
    output = output + jnp.einsum('hij,hje->hie', attend, update, precision=precise)
    state = decay_end[..., None] * state + jnp.einsum('hcd,hce->hde', keys_end, update, precision=precise)
    return (state, output)

def finish(core, gate_value, norm_gain, count):
    scaled = core * lax.rsqrt(lax.optimization_barrier(jnp.mean(core * core, axis=-1, keepdims=True)) + 1e-06) * norm_gain
    return (scaled.reshape(count, H * DK) * gate_value).astype(jnp.bfloat16)

def reference(tokens, qkv_weight, conv_weight, decay_down, decay_up, decay_rate, beta_weight, beta_scale, gate_down, gate_up, norm_gain):
    count = tokens.shape[0]
    mixed = jnp.dot(tokens.astype(jnp.float32), qkv_weight.astype(jnp.float32), preferred_element_type=jnp.float32).astype(jnp.bfloat16)
    padded = jnp.concatenate([jnp.zeros((CONV - 1, mixed.shape[1]), jnp.bfloat16), mixed], axis=0)
    query, keys, values = features(padded, count, conv_weight)
    beta, logdec, gate_value = gates(tokens, decay_down, decay_up, decay_rate, beta_weight, beta_scale, gate_down, gate_up)
    beta_blocks = beta.reshape(count // BLOCK, BLOCK, H).transpose(0, 2, 1)
    terms = block_terms(to_blocks(query, count), to_blocks(keys, count), to_blocks(values, count), beta_blocks, to_blocks(logdec.reshape(count, H, DK), count))
    initial = jnp.zeros((H, DK, DK), jnp.float32)
    final_state, outputs = lax.scan(advance, initial, terms)
    core = outputs.transpose(0, 2, 1, 3).reshape(count, H, DK)
    return finish(core, gate_value, norm_gain, count)
```

```python
import functools

import jax
import jax.numpy as jnp
import numpy as np
from jax import lax
from jax.experimental import pallas as pl
from jax.experimental.pallas import tpu as pltpu
from jax.sharding import Mesh
from jax.sharding import PartitionSpec as P

H = 16
DK = 128
CONV = 4
D = 2304
HV = H * DK
BF = jnp.bfloat16
F32 = jnp.float32

NZ, NX, NC, NY = 4, 4, 2, 4
ROW = NX * NC
SHARD = 128
GROUP = ROW * SHARD
QUART = D // NY
UNIT = 64
PACK = QUART // 2
HALF = PACK // 2
VMEM_LIMIT = 56 * 1024 * 1024


def unit_plan():
    count = NZ * ROW
    units = 3 * HV // UNIT
    dest = {}
    for u in range(units):
        kind, rest = divmod(u, HV // UNIT)
        head, half = divmod(rest, 2)
        dest[u] = (((head % 2) * 2 + half) * ROW + head // 2, kind)
    left = {i: [3 * i, 3 * i + 1, 3 * i + 2] for i in range(count)}
    sends, routes = [], []
    arrival = np.zeros((count, 3), np.int32)
    for r in range(3):
        owner = {}

        def place(i, seen):
            for u in left[i]:
                d = dest[u][0]
                if d in seen:
                    continue
                seen.add(d)
                if d not in owner or place(owner[d][0], seen):
                    owner[d] = (i, u)
                    return True
            return False

        for i in range(count):
            assert place(i, set())
        table = np.zeros(count, np.int32)
        route = []
        for d, (i, u) in owner.items():
            table[i] = u - 3 * i
            arrival[d, dest[u][1]] = r
            route.append((i, d))
            left[i].remove(u)
        sends.append(table)
        routes.append(sorted(route))
    order = arrival.reshape(NZ, ROW, 3).transpose(1, 0, 2).reshape(ROW, NZ * 3)
    return sends, routes, order


SENDS, ROUTES, ORDER = unit_plan()


def ring(distance, size=4):
    return [(i, (i + distance) % size) for i in range(size)]


def ahead(distance, size=4):
    return [(i, i + distance) for i in range(size - distance)]


def split(x):
    high = x.astype(BF)
    return high, (x - high.astype(F32)).astype(BF)


def dot(a, b):
    return lax.dot_general(a, b, (((1,), (0,)), ((), ())), preferred_element_type=F32)


def dot_nt(a, b):
    return lax.dot_general(a, b, (((1,), (1,)), ((), ())), preferred_element_type=F32)


def mm3(a, b):
    ah, al = split(a)
    bh, bl = split(b)
    return dot(jnp.concatenate([ah, al, ah], axis=1), jnp.concatenate([bh, bh, bl], axis=0))


def mm3_nt(a, b):
    ah, al = split(a)
    bh, bl = split(b)
    return dot_nt(jnp.concatenate([ah, al, ah], axis=1), jnp.concatenate([bh, bh, bl], axis=1))


def sigmoid(x):
    return 1.0 / (1.0 + jnp.exp(-x))


def unit_lower_inverse(a, rows, cols):
    eye = jnp.where(rows == cols, 1.0, 0.0)
    inverse = eye - jnp.where((rows // 2) == (cols // 2), a, 0.0)
    size = 2
    while size < SHARD:
        band = ((rows // (2 * size)) == (cols // (2 * size))) & ((rows // size) != (cols // size))
        low = jnp.where(band, a, 0.0).astype(BF)
        near = inverse.astype(BF)
        inverse = inverse - dot(dot(near, low).astype(BF), near)
        size *= 2
    near = inverse.astype(BF)
    ah, al = split(a)
    rest = (
        eye
        - near.astype(F32)
        - dot(jnp.concatenate([ah, al], axis=1), jnp.concatenate([near, near], axis=0))
    )
    return near.astype(F32) + dot(near, rest.astype(BF))


def block_kernel(
    sp,
    own,
    oth,
    halo,
    wsmall,
    decay_up,
    gate_up,
    rate,
    beta_scale,
    conv_q,
    conv_k,
    conv_v,
    *rest,
):
    parts = rest[:8]
    qeff_o, core_o, gate_o, state_o = rest[8:12]
    abuf, bbuf, wbuf, mbuf, tbuf, state, sems = rest[12:]
    step = pl.program_id(0)
    z, c, y, g = sp[0], sp[1], sp[2], sp[3]

    @pl.when(step == 0)
    def _():
        copies = []
        for k in range(4):
            copies.append(
                pltpu.make_async_copy(parts[k], abuf.at[lax.rem(y - k + 4, 4)], sems.at[k])
            )
            copies.append(
                pltpu.make_async_copy(parts[4 + k], bbuf.at[lax.rem(z - k + 4, 4)], sems.at[4 + k])
            )
        for copy in copies:
            copy.start()
        for copy in copies:
            copy.wait()

        def place(row, kind, hp, first, second):
            cols = pl.ds(kind * 256 + hp * 128, 128)
            wbuf[pl.ds(row, HALF), cols] = jnp.concatenate(
                [first[:, :UNIT], second[:, :UNIT]], axis=1
            )
            wbuf[pl.ds(row + PACK, HALF), cols] = jnp.concatenate(
                [first[:, UNIT:], second[:, UNIT:]], axis=1
            )

        for yy in range(4):
            ky = lax.rem(y - yy + 4, 4)
            for kind in range(3):
                for hp in range(2):
                    pa, pb = [], []
                    for half in range(2):
                        zz = 2 * hp + half
                        kz = lax.rem(z - zz + 4, 4)
                        order = sp[4 + 3 * zz + kind]
                        pa.append(abuf[yy, kz, order])
                        pb.append(bbuf[zz, ky, order])
                    place(QUART * yy, kind, hp, *pa)
                    place(QUART * yy + HALF, kind, hp, *pb)
        before = dot(halo[...], wbuf[...]).astype(BF).astype(F32)
        mbuf[0:8] = before[8:16]
        rr = lax.broadcasted_iota(jnp.int32, (DK, 2 * DK), 0)
        cc = lax.broadcasted_iota(jnp.int32, (DK, 2 * DK), 1)
        start = jnp.where(rr == cc, 1.0, 0.0)
        state[0] = start
        state[1] = start

    @pl.when(c == 0)
    def _():
        tbuf[0:SHARD] = own[0]
        tbuf[SHARD:] = oth[0]

    @pl.when(c != 0)
    def _():
        tbuf[0:SHARD] = oth[0]
        tbuf[SHARD:] = own[0]

    tok = tbuf[...]
    small = dot(tok, wsmall[...])
    decay_low = small[:, :128].astype(BF)
    gate_low = small[:, 128:256].astype(BF)
    beta_all = beta_scale[...] * sigmoid(small[:, 256:])
    logdec = -rate[...] * sigmoid(dot(decay_low, decay_up[...]))
    gate_o[...] = sigmoid(dot(gate_low, gate_up[...]))
    mbuf[8:] = dot(tok, wbuf[...]).astype(BF).astype(F32)

    def active(kind, taps):
        cols = slice(256 * kind, 256 * kind + 256)
        total = taps[0:1] * mbuf[5 : 5 + 256, cols]
        for j in range(1, CONV):
            total = total + taps[j : j + 1] * mbuf[5 + j : 5 + j + 256, cols]
        return total * sigmoid(total)

    query = active(0, conv_q)
    keys = active(1, conv_k)
    values = active(2, conv_v)
    mbuf[0:8] = mbuf[256:264]

    rows = lax.broadcasted_iota(jnp.int32, (SHARD, SHARD), 0)
    cols = lax.broadcasted_iota(jnp.int32, (SHARD, SHARD), 1)
    ones_low = jnp.where(rows >= cols, 1.0, 0.0).astype(BF)
    lane = lax.broadcasted_iota(jnp.int32, (SHARD, 128), 1)
    for h in range(2):
        hs = slice(DK * h, DK * h + DK)
        for blk in range(2):
            ts = slice(SHARD * blk, SHARD * blk + SHARD)
            q, k, v = query[ts, hs], keys[ts, hs], values[ts, hs]
            q = q * (lax.rsqrt(jnp.sum(q * q, axis=1, keepdims=True) + 1e-06) * DK**-0.5)
            k = k * lax.rsqrt(jnp.sum(k * k, axis=1, keepdims=True) + 1e-06)
            beta = jnp.sum(
                jnp.where(lane == 2 * g + h, beta_all[ts], 0.0), axis=1, keepdims=True
            )
            lh, ll = split(logdec[ts, hs])
            log_sum = dot(
                jnp.concatenate([ones_low, ones_low], axis=1), jnp.concatenate([lh, ll], axis=0)
            )
            grow = jnp.exp(log_sum)
            end = log_sum[SHARD - 1 : SHARD]
            k_up = k * grow
            k_down = k * jnp.exp(-log_sum)
            q_up = q * grow
            k_end = k * jnp.exp(end - log_sum)
            both = mm3_nt(jnp.concatenate([k_up, q_up], axis=0), k_down)
            system = jnp.where(rows > cols, both[:SHARD], 0.0) * beta
            attend = jnp.where(rows >= cols, both[SHARD:], 0.0)
            inverse = unit_lower_inverse(system, rows, cols)
            solved = mm3(inverse, jnp.concatenate([k_up, v], axis=1) * beta)
            mixed = mm3(jnp.concatenate([attend, k_end.T], axis=0), solved)
            q_full = q_up - mixed[:SHARD, :DK]
            step_matrix = jnp.where(rows == cols, jnp.exp(end), 0.0) - mixed[SHARD:, :DK]
            carry = state[h]
            out = mm3(jnp.concatenate([q_full, step_matrix], axis=0), carry)
            qeff_o[ts, hs] = out[:SHARD, :DK]
            core_o[ts, hs] = out[:SHARD, DK:] + mixed[:SHARD, DK:]
            state[h, :, :DK] = out[SHARD:, :DK]
            state[h, :, DK:] = out[SHARD:, DK:] + mixed[SHARD:, DK:]

    @pl.when(step == pl.num_programs(0) - 1)
    def _():
        state_o[...] = state[...]


def run_blocks(sp, own, oth, halo, wsmall, decay_up, gate_up, rate, beta_scale, conv, parts):
    def fixed(shape):
        return pl.BlockSpec(shape, lambda i, s: (0,) * len(shape))

    def by_group(shape, offset=0):
        return pl.BlockSpec(shape, lambda i, s: (0, s[3] + offset))

    steps = NX
    token_spec = pl.BlockSpec((1, SHARD, D), lambda i, s: (i, 0, 0))
    out_spec = pl.BlockSpec((2 * SHARD, 2 * DK), lambda i, s: (i, 0))
    big = jax.ShapeDtypeStruct((GROUP, 2 * DK), F32)
    return pl.pallas_call(
        block_kernel,
        name="block_terms",
        out_shape=(big, big, big, jax.ShapeDtypeStruct((2, DK, 2 * DK), F32)),
        grid_spec=pltpu.PrefetchScalarGridSpec(
            num_scalar_prefetch=1,
            grid=(steps,),
            in_specs=[
                token_spec,
                token_spec,
                fixed((16, D)),
                fixed((D, 384)),
                by_group((128, 256)),
                by_group((128, 256)),
                by_group((1, 256)),
                fixed((1, 128)),
                by_group((CONV, 256)),
                by_group((CONV, 256), 8),
                by_group((CONV, 256), 16),
            ]
            + [pl.BlockSpec(memory_space=pl.ANY)] * 8,
            out_specs=[out_spec, out_spec, out_spec, fixed((2, DK, 2 * DK))],
            scratch_shapes=[
                pltpu.VMEM((4, 4, 3, HALF, 128), BF),
                pltpu.VMEM((4, 4, 3, HALF, 128), BF),
                pltpu.VMEM((D, 768), BF),
                pltpu.VMEM((8 + 2 * SHARD, 768), F32),
                pltpu.VMEM((2 * SHARD, D), BF),
                pltpu.VMEM((2, DK, 2 * DK), F32),
                pltpu.SemaphoreType.DMA((8,)),
            ],
        ),
        compiler_params=pltpu.CompilerParams(vmem_limit_bytes=VMEM_LIMIT),
    )(
        sp, own, oth, halo, wsmall, decay_up, gate_up, rate, beta_scale, conv, conv, conv, *parts
    )


def finish_kernel(near, middle, far, qeff, core, gate, gain, out, state):
    @pl.when(pl.program_id(0) == 0)
    def _():
        for h in range(2):
            carry = middle[h, :, DK:] + mm3(middle[h, :, :DK], far[h])
            state[h] = near[h, :, DK:] + mm3(near[h, :, :DK], carry)

    for h in range(2):
        hs = slice(DK * h, DK * h + DK)
        full = core[:, hs] + mm3(qeff[:, hs], state[h])
        scale = lax.rsqrt(jnp.mean(full * full, axis=1, keepdims=True) + 1e-06)
        out[:, hs] = (full * scale * gain[...] * gate[:, hs]).astype(BF)


def run_finish(near, middle, far, qeff, core, gate, gain):
    def fixed(shape):
        return pl.BlockSpec(shape, lambda i: (0,) * len(shape))

    tile = pl.BlockSpec((256, 2 * DK), lambda i: (i, 0))
    return pl.pallas_call(
        finish_kernel,
        name="finish",
        out_shape=jax.ShapeDtypeStruct((GROUP, 2 * DK), BF),
        grid=(GROUP // 256,),
        in_specs=[
            fixed((2, DK, 2 * DK)),
            fixed((2, DK, 2 * DK)),
            fixed((2, DK, DK)),
            tile,
            tile,
            tile,
            fixed((1, DK)),
        ],
        out_specs=tile,
        scratch_shapes=[pltpu.VMEM((2, DK, DK), F32)],
        compiler_params=pltpu.CompilerParams(vmem_limit_bytes=VMEM_LIMIT),
    )(near, middle, far, qeff, core, gate, gain)


def gather_weights(weight, z, place, y):
    quarter = lax.dynamic_slice(weight, (QUART * y, 0), (QUART, 3 * UNIT))
    units = jnp.stack(
        [
            jnp.concatenate(
                [
                    quarter[:PACK, UNIT * k : UNIT * k + UNIT],
                    quarter[PACK:, UNIT * k : UNIT * k + UNIT],
                ],
                axis=1,
            )
            for k in range(3)
        ]
    )
    arrived = []
    for table, route in zip(SENDS, ROUTES):
        unit = lax.dynamic_index_in_dim(units, jnp.asarray(table)[place], 0, keepdims=False)
        arrived.append(lax.ppermute(unit, ("z", "x", "c"), route))
    mine = jnp.stack(arrived)

    def spread(block, axis):
        return [block] + [lax.ppermute(block, axis, ring(k)) for k in range(1, 4)]

    upper, lower = mine[:, :HALF], mine[:, HALF:]
    upper_z, lower_y = jnp.stack(spread(upper, "z")), jnp.stack(spread(lower, "y"))
    return spread(upper_z, "y") + spread(lower_y, "z")


def per_device(
    tokens,
    qkv_weight,
    conv_weight,
    decay_down,
    decay_up,
    decay_rate,
    beta_weight,
    beta_scale,
    gate_down,
    gate_up,
    norm_gain,
):
    z, x, c, y = (lax.axis_index(a) for a in ("z", "x", "c", "y"))
    g = x * NC + c
    own = lax.all_gather(tokens, "x", axis=0)
    parts = gather_weights(qkv_weight, z, z * ROW + g, y)
    oth = lax.ppermute(own, "c", [(0, 1), (1, 0)])
    last = jnp.where(c == NC - 1, own[NX - 1, SHARD - 16 :], oth[NX - 1, SHARD - 16 :])
    halo = lax.ppermute(last, "z", ahead(1))
    wsmall = jnp.concatenate(
        [decay_down, gate_down, jnp.pad(beta_weight, ((0, 0), (0, 128 - H)))], axis=1
    )
    sp = jnp.concatenate(
        [jnp.stack([z, c, y, g]).astype(jnp.int32), jnp.asarray(ORDER)[g].astype(jnp.int32)]
    )
    qeff, core, gate, state = run_blocks(
        sp,
        own,
        oth,
        halo,
        wsmall,
        decay_up,
        gate_up,
        decay_rate.reshape(1, HV),
        jnp.pad(beta_scale, (0, 128 - H)).reshape(1, 128),
        conv_weight,
        parts,
    )
    near = lax.ppermute(state, "z", ahead(1))
    middle = lax.ppermute(state, "z", ahead(2))
    far = lax.ppermute(state[:, :, DK:], "z", ahead(3))
    out = run_finish(near, middle, far, qeff, core, gate, norm_gain.reshape(1, DK))
    out = lax.all_to_all(out.reshape(ROW, SHARD, 2 * DK), ("x", "c"), 0, 0)
    return out.transpose(1, 0, 2).reshape(SHARD, HV)


def solution(mesh):
    fine = Mesh(mesh.devices.reshape(NZ, NX, NC, NY), ("z", "x", "c", "y"))
    seq = ("z", "x", "c")
    in_specs = (P(("y",) + seq, None), P(None, seq)) + (P(),) * 9
    return jax.shard_map(
        per_device,
        mesh=fine,
        in_specs=in_specs,
        out_specs=P(("y",) + seq, None),
        check_vma=False,
    )
```

```python
import functools

import jax
import jax.numpy as jnp
import numpy as np
from jax import lax
from jax.experimental import pallas as pl
from jax.experimental.pallas import tpu as pltpu
from jax.sharding import Mesh
from jax.sharding import PartitionSpec as P

H = 16
DK = 128
CONV = 4
D = 2304
HV = H * DK
BF = jnp.bfloat16
F32 = jnp.float32

NZ, NX, NC, NY = 4, 4, 2, 4
ROW = NX * NC
SHARD = 128
GROUP = ROW * SHARD
UNIT = 64
PACK = D // 2
HALF = PACK // 2
STEP = 2 * SHARD
VMEM_LIMIT = 56 * 1024 * 1024


def unit_plan():
    count = NZ * ROW
    units = 3 * HV // UNIT
    dest = {}
    for u in range(units):
        kind, rest = divmod(u, HV // UNIT)
        head, half = divmod(rest, 2)
        dest[u] = (((head % 2) * 2 + half) * ROW + head // 2, kind)
    left = {i: [3 * i, 3 * i + 1, 3 * i + 2] for i in range(count)}
    sends, routes = [], []
    arrival = np.zeros((count, 3), np.int32)
    for r in range(3):
        owner = {}

        def place(i, seen):
            for u in left[i]:
                d = dest[u][0]
                if d in seen:
                    continue
                seen.add(d)
                if d not in owner or place(owner[d][0], seen):
                    owner[d] = (i, u)
                    return True
            return False

        for i in range(count):
            assert place(i, set())
        table = np.zeros(count, np.int32)
        route = []
        for d, (i, u) in owner.items():
            table[i] = u - 3 * i
            arrival[d, dest[u][1]] = r
            route.append((i, d))
            left[i].remove(u)
        sends.append(table)
        routes.append(sorted(route))
    order = arrival.reshape(NZ, ROW, 3).transpose(1, 0, 2).reshape(ROW, NZ * 3)
    return sends, routes, order


SENDS, ROUTES, ORDER = unit_plan()


def ring(distance, size=4):
    return [(i, (i + distance) % size) for i in range(size)]


def ahead(distance, size=4):
    return [(i, i + distance) for i in range(size - distance)]


def split(x):
    high = x.astype(BF)
    return high, (x - high.astype(F32)).astype(BF)


def dot(a, b):
    return lax.dot_general(a, b, (((1,), (0,)), ((), ())), preferred_element_type=F32)


def dot_nt(a, b):
    return lax.dot_general(a, b, (((1,), (1,)), ((), ())), preferred_element_type=F32)


def mm3(a, b):
    ah, al = split(a)
    bh, bl = split(b)
    return dot(jnp.concatenate([ah, al, ah], axis=1), jnp.concatenate([bh, bh, bl], axis=0))


def mm3_nt(a, b):
    ah, al = split(a)
    bh, bl = split(b)
    return dot_nt(jnp.concatenate([ah, al, ah], axis=1), jnp.concatenate([bh, bh, bl], axis=1))


def sigmoid(x):
    return 1.0 / (1.0 + jnp.exp(-x))


def unit_lower_inverses(systems, rows, cols):
    eye = jnp.where(rows == cols, 1.0, 0.0)
    pair = (rows // 2) == (cols // 2)
    found = [eye - jnp.where(pair, a, 0.0) for a in systems]
    size = 2
    while size < SHARD:
        band = ((rows // (2 * size)) == (cols // (2 * size))) & ((rows // size) != (cols // size))
        low = [jnp.where(band, a, 0.0).astype(BF) for a in systems]
        near = [t.astype(BF) for t in found]
        half = [dot(t, a).astype(BF) for t, a in zip(near, low)]
        step = [dot(p, t) for p, t in zip(half, near)]
        found = [t - s for t, s in zip(found, step)]
        size *= 2
    near = [t.astype(BF) for t in found]
    parts = [jnp.concatenate(split(a), axis=1) for a in systems]
    rest = [
        eye - t.astype(F32) - dot(a, jnp.concatenate([t, t], axis=0)) for a, t in zip(parts, near)
    ]
    return [t.astype(F32) + dot(t, r.astype(BF)) for t, r in zip(near, rest)]


def fixed(shape):
    return pl.BlockSpec(shape, lambda i, s: (0,) * len(shape))


def by_group(shape, offset=0):
    return pl.BlockSpec(shape, lambda i, s: (0, s[2] + offset))


def by_step(columns):
    return pl.BlockSpec((STEP, columns), lambda i, s: (i, 0))


def params():
    return pltpu.CompilerParams(vmem_limit_bytes=VMEM_LIMIT)


def cost(flops, size):
    return pl.CostEstimate(flops=int(flops), bytes_accessed=int(size), transcendentals=0)


def gate_kernel(sp, tokens, wsmall, decay_up, gate_up, rate, scale, log_o, beta_o, gate_o):
    g = sp[2]
    small = dot(tokens[...], wsmall[...])
    decay_low = small[:, :128].astype(BF)
    gate_low = small[:, 128:256].astype(BF)
    beta_all = scale[...] * sigmoid(small[:, 256:])
    logdec = -rate[...] * sigmoid(dot(decay_low, decay_up[...]))
    gate_o[...] = sigmoid(dot(gate_low, gate_up[...]))
    rows = lax.broadcasted_iota(jnp.int32, (SHARD, SHARD), 0)
    cols = lax.broadcasted_iota(jnp.int32, (SHARD, SHARD), 1)
    ones_low = jnp.where(rows >= cols, 1.0, 0.0).astype(BF)
    ones_twice = jnp.concatenate([ones_low, ones_low], axis=1)
    high, low = split(logdec)
    for blk in range(STEP // SHARD):
        ts = slice(SHARD * blk, SHARD * blk + SHARD)
        log_o[ts] = dot(ones_twice, jnp.concatenate([high[ts], low[ts]], axis=0))
    lane = lax.broadcasted_iota(jnp.int32, (STEP, 128), 1)
    for h in range(2):
        mine = jnp.sum(jnp.where(lane == 2 * g + h, beta_all, 0.0), axis=1, keepdims=True)
        beta_o[:, DK * h : DK * h + DK] = jnp.broadcast_to(mine, (STEP, DK))


def run_gates(sp, tokens, wsmall, decay_up, gate_up, rate, scale):
    wide = jax.ShapeDtypeStruct((GROUP, 2 * DK), F32)
    return pl.pallas_call(
        gate_kernel,
        name="block_gates",
        out_shape=(wide, wide, wide),
        grid_spec=pltpu.PrefetchScalarGridSpec(
            num_scalar_prefetch=1,
            grid=(GROUP // STEP,),
            in_specs=[
                by_step(D),
                fixed((D, 384)),
                by_group((128, 256)),
                by_group((128, 256)),
                by_group((1, 256)),
                fixed((1, 128)),
            ],
            out_specs=[by_step(2 * DK)] * 3,
        ),
        compiler_params=params(),
        cost_estimate=cost(2e9, 1e7),
    )(sp, tokens, wsmall, decay_up, gate_up, rate, scale)


def active(mixed, cols, taps):
    total = taps[0:1] * mixed[5 : 5 + STEP, cols]
    for j in range(1, CONV):
        total = total + taps[j : j + 1] * mixed[5 + j : 5 + j + STEP, cols]
    return total * sigmoid(total)


def state_kernel(sp, tokens, halo, log_sums, betas, conv_k, conv_v, *rest):
    parts = rest[:8]
    down_o, solved_o, carry_o, wq_o, state_o = rest[8:13]
    abuf, bbuf, wbuf, mixed, state, sems = rest[13:]
    step = pl.program_id(0)
    z, y = sp[0], sp[1]

    @pl.when(step == 0)
    def _():
        copies = []
        for k in range(4):
            copies.append(
                pltpu.make_async_copy(parts[k], abuf.at[lax.rem(y - k + 4, 4)], sems.at[k])
            )
            copies.append(
                pltpu.make_async_copy(parts[4 + k], bbuf.at[lax.rem(z - k + 4, 4)], sems.at[4 + k])
            )
        for copy in copies:
            copy.start()
        for copy in copies:
            copy.wait()

        def place(row, kind, hp, first, second):
            target = wq_o if kind == 0 else wbuf
            cols = pl.ds((kind - 1 if kind else 0) * 256 + hp * 128, 128)
            target[pl.ds(row, HALF), cols] = jnp.concatenate(
                [first[:, :UNIT], second[:, :UNIT]], axis=1
            )
            target[pl.ds(row + PACK, HALF), cols] = jnp.concatenate(
                [first[:, UNIT:], second[:, UNIT:]], axis=1
            )

        for kind in range(3):
            for hp in range(2):
                pa, pb = [], []
                for half in range(2):
                    zz = 2 * hp + half
                    kz = lax.rem(z - zz + 4, 4)
                    plane = sp[3 + 3 * zz + kind]
                    pa.append(abuf[plane, kz])
                    pb.append(bbuf[zz, plane])
                place(0, kind, hp, *pa)
                place(HALF, kind, hp, *pb)
        before = dot(halo[...], wbuf[...]).astype(BF).astype(F32)
        mixed[0:8] = before[8:16]
        rr = lax.broadcasted_iota(jnp.int32, (DK, 2 * DK), 0)
        cc = lax.broadcasted_iota(jnp.int32, (DK, 2 * DK), 1)
        start = jnp.where(rr == cc, 1.0, 0.0)
        state[0] = start
        state[1] = start

    mixed[8:] = dot(tokens[...], wbuf[...]).astype(BF).astype(F32)
    keys = active(mixed, slice(0, 256), conv_k)
    values = active(mixed, slice(256, 512), conv_v)
    mixed[0:8] = mixed[STEP : STEP + 8]

    rows = lax.broadcasted_iota(jnp.int32, (SHARD, SHARD), 0)
    cols = lax.broadcasted_iota(jnp.int32, (SHARD, SHARD), 1)
    places = [
        (h, blk, slice(SHARD * blk, SHARD * blk + SHARD), slice(DK * h, DK * h + DK))
        for blk in range(STEP // SHARD)
        for h in range(2)
    ]
    systems, sides, ends, tails = [], [], [], []
    for h, blk, ts, hs in places:
        k, beta, log_sum = keys[ts, hs], betas[ts, hs], log_sums[ts, hs]
        k = k * lax.rsqrt(jnp.sum(k * k, axis=1, keepdims=True) + 1e-06)
        end = log_sum[SHARD - 1 : SHARD]
        k_up = k * jnp.exp(log_sum)
        k_down = k * jnp.exp(-log_sum)
        down_o[ts, hs] = k_down
        systems.append(jnp.where(rows > cols, mm3_nt(k_up, k_down), 0.0) * beta)
        sides.append(jnp.concatenate([k_up * beta, values[ts, hs] * beta], axis=1))
        ends.append((k * jnp.exp(end - log_sum)).T)
        tails.append(jnp.where(rows == cols, jnp.exp(end), 0.0))
    inverses = unit_lower_inverses(systems, rows, cols)
    solved = [mm3(t, r) for t, r in zip(inverses, sides)]
    moves = [mm3(e, s) for e, s in zip(ends, solved)]
    for (h, blk, ts, hs), tail, sol, move in zip(places, tails, solved, moves):
        solved_o[ts, 2 * DK * h : 2 * DK * h + 2 * DK] = sol
        carry = state[h]
        carry_o[ts, 2 * DK * h : 2 * DK * h + 2 * DK] = carry
        new = mm3(tail - move[:, :DK], carry)
        state[h, :, :DK] = new[:, :DK]
        state[h, :, DK:] = new[:, DK:] + move[:, DK:]

    @pl.when(step == pl.num_programs(0) - 1)
    def _():
        state_o[...] = state[...]


def run_state(sp, tokens, halo, log_sums, betas, conv, parts):
    return pl.pallas_call(
        state_kernel,
        name="block_state",
        out_shape=(
            jax.ShapeDtypeStruct((GROUP, 2 * DK), F32),
            jax.ShapeDtypeStruct((GROUP, 4 * DK), F32),
            jax.ShapeDtypeStruct((GROUP, 4 * DK), F32),
            jax.ShapeDtypeStruct((D, 2 * DK), BF),
            jax.ShapeDtypeStruct((2, DK, 2 * DK), F32),
        ),
        grid_spec=pltpu.PrefetchScalarGridSpec(
            num_scalar_prefetch=1,
            grid=(GROUP // STEP,),
            in_specs=[
                by_step(D),
                fixed((16, D)),
                by_step(2 * DK),
                by_step(2 * DK),
                by_group((CONV, 256), 8),
                by_group((CONV, 256), 16),
            ]
            + [pl.BlockSpec(memory_space=pl.ANY)] * 8,
            out_specs=[
                by_step(2 * DK),
                by_step(4 * DK),
                by_step(4 * DK),
                fixed((D, 2 * DK)),
                fixed((2, DK, 2 * DK)),
            ],
            scratch_shapes=[
                pltpu.VMEM((NY, NZ, HALF, 128), BF),
                pltpu.VMEM((NZ, 3, HALF, 128), BF),
                pltpu.VMEM((D, 512), BF),
                pltpu.VMEM((8 + STEP, 512), F32),
                pltpu.VMEM((2, DK, 2 * DK), F32),
                pltpu.SemaphoreType.DMA((8,)),
            ],
        ),
        compiler_params=params(),
        cost_estimate=cost(1e10, 2e7),
    )(sp, tokens, halo, log_sums, betas, conv, conv, *parts)


def query_kernel(
    sp, tokens, halo, wq, conv_q, log_sums, k_downs, solved, carries, qeff_o, core_o, mixed
):
    @pl.when(pl.program_id(0) == 0)
    def _():
        before = dot(halo[...], wq[...]).astype(BF).astype(F32)
        mixed[0:8] = before[8:16]

    mixed[8:] = dot(tokens[...], wq[...]).astype(BF).astype(F32)
    query = active(mixed, slice(0, 256), conv_q)
    mixed[0:8] = mixed[STEP : STEP + 8]
    rows = lax.broadcasted_iota(jnp.int32, (SHARD, SHARD), 0)
    cols = lax.broadcasted_iota(jnp.int32, (SHARD, SHARD), 1)
    for blk in range(STEP // SHARD):
        for h in range(2):
            ts = slice(SHARD * blk, SHARD * blk + SHARD)
            hs = slice(DK * h, DK * h + DK)
            both = slice(2 * DK * h, 2 * DK * h + 2 * DK)
            q = query[ts, hs]
            q = q * (lax.rsqrt(jnp.sum(q * q, axis=1, keepdims=True) + 1e-06) * DK**-0.5)
            q_up = q * jnp.exp(log_sums[ts, hs])
            attend = jnp.where(rows >= cols, mm3_nt(q_up, k_downs[ts, hs]), 0.0)
            within = mm3(attend, solved[ts, both])
            out = mm3(q_up - within[:, :DK], carries[ts, both])
            qeff_o[ts, hs] = out[:, :DK]
            core_o[ts, hs] = out[:, DK:] + within[:, DK:]


def run_queries(sp, tokens, halo, wq, conv, log_sums, k_downs, solved, carries):
    wide = jax.ShapeDtypeStruct((GROUP, 2 * DK), F32)
    return pl.pallas_call(
        query_kernel,
        name="block_query",
        out_shape=(wide, wide),
        grid_spec=pltpu.PrefetchScalarGridSpec(
            num_scalar_prefetch=1,
            grid=(GROUP // STEP,),
            in_specs=[
                by_step(D),
                fixed((16, D)),
                fixed((D, 2 * DK)),
                by_group((CONV, 256)),
                by_step(2 * DK),
                by_step(2 * DK),
                by_step(4 * DK),
                by_step(4 * DK),
            ],
            out_specs=[by_step(2 * DK)] * 2,
            scratch_shapes=[pltpu.VMEM((8 + STEP, 256), F32)],
        ),
        compiler_params=params(),
        cost_estimate=cost(5e9, 2e7),
    )(sp, tokens, halo, wq, conv, log_sums, k_downs, solved, carries)


def finish_kernel(near, middle, far, qeff, core, gate, gain, out, state):
    @pl.when(pl.program_id(0) == 0)
    def _():
        for h in range(2):
            carry = middle[h, :, DK:] + mm3(middle[h, :, :DK], far[h])
            state[h] = near[h, :, DK:] + mm3(near[h, :, :DK], carry)

    for h in range(2):
        hs = slice(DK * h, DK * h + DK)
        full = core[:, hs] + mm3(qeff[:, hs], state[h])
        scale = lax.rsqrt(jnp.mean(full * full, axis=1, keepdims=True) + 1e-06)
        out[:, hs] = (full * scale * gain[...] * gate[:, hs]).astype(BF)


def run_finish(near, middle, far, qeff, core, gate, gain):
    def whole(shape):
        return pl.BlockSpec(shape, lambda i: (0,) * len(shape))

    tile = pl.BlockSpec((256, 2 * DK), lambda i: (i, 0))
    return pl.pallas_call(
        finish_kernel,
        name="finish",
        out_shape=jax.ShapeDtypeStruct((GROUP, 2 * DK), BF),
        grid=(GROUP // 256,),
        in_specs=[
            whole((2, DK, 2 * DK)),
            whole((2, DK, 2 * DK)),
            whole((2, DK, DK)),
            tile,
            tile,
            tile,
            whole((1, DK)),
        ],
        out_specs=tile,
        scratch_shapes=[pltpu.VMEM((2, DK, DK), F32)],
        compiler_params=pltpu.CompilerParams(vmem_limit_bytes=VMEM_LIMIT),
    )(near, middle, far, qeff, core, gate, gain)


def gather_weights(weight, spot, y):
    sent = jnp.asarray(np.stack(SENDS))[jnp.minimum(y, 2), spot]
    units = [weight[:, UNIT * k : UNIT * k + UNIT] for k in range(3)]
    unit = jnp.where(sent == 0, units[0], jnp.where(sent == 1, units[1], units[2]))
    packed = jnp.concatenate([unit[:PACK], unit[PACK:]], axis=1)
    route = [(i * NY + r, d * NY + r) for r in range(3) for i, d in ROUTES[r]]
    mine = lax.ppermute(packed, ("z", "x", "c", "y"), route)
    from_planes = [[(i, (i + k) % NY) for i in range(3)] for k in range(4)]
    upper, lower = mine[:HALF], mine[HALF:]
    upper_z = jnp.stack([upper] + [lax.ppermute(upper, "z", ring(k)) for k in range(1, 4)])
    lower_y = jnp.stack([lower] + [lax.ppermute(lower, "y", from_planes[k]) for k in range(1, 4)])
    lower_y = jnp.stack(
        [
            lax.dynamic_index_in_dim(lower_y, lax.rem(y - plane + NY, NY), 0, keepdims=False)
            for plane in range(3)
        ]
    )
    upper_z, lower_y = lax.optimization_barrier((upper_z, lower_y))
    return (
        [upper_z]
        + [lax.ppermute(upper_z, "y", from_planes[k]) for k in range(1, 4)]
        + [lower_y]
        + [lax.ppermute(lower_y, "z", ring(k)) for k in range(1, 4)]
    )


def per_device(
    tokens,
    qkv_weight,
    conv_weight,
    decay_down,
    decay_up,
    decay_rate,
    beta_weight,
    beta_scale,
    gate_down,
    gate_up,
    norm_gain,
):
    z, x, c, y = (lax.axis_index(a) for a in ("z", "x", "c", "y"))
    g = x * NC + c
    row = lax.all_gather(tokens, ("x", "c"), axis=0, tiled=True)
    parts = gather_weights(qkv_weight, z * ROW + g, y)
    halo = lax.ppermute(row[GROUP - 16 :], "z", ahead(1))
    wsmall = jnp.concatenate(
        [decay_down, gate_down, jnp.pad(beta_weight, ((0, 0), (0, 128 - H)))], axis=1
    )
    sp = jnp.concatenate(
        [jnp.stack([z, y, g]).astype(jnp.int32), jnp.asarray(ORDER)[g].astype(jnp.int32)]
    )
    log_sums, betas, gate = run_gates(
        sp,
        row,
        wsmall,
        decay_up,
        gate_up,
        decay_rate.reshape(1, HV),
        jnp.pad(beta_scale, (0, 128 - H)).reshape(1, 128),
    )
    k_downs, solved, carries, wq, state = run_state(
        sp, row, halo, log_sums, betas, conv_weight, parts
    )
    near = lax.ppermute(state, "z", ahead(1))
    middle = lax.ppermute(state, "z", ahead(2))
    far = lax.ppermute(state[:, :, DK:], "z", ahead(3))
    qeff, core = run_queries(sp, row, halo, wq, conv_weight, log_sums, k_downs, solved, carries)
    out = run_finish(near, middle, far, qeff, core, gate, norm_gain.reshape(1, DK))
    out = lax.all_to_all(out.reshape(ROW, SHARD, 2 * DK), ("x", "c"), 0, 0)
    return out.transpose(1, 0, 2).reshape(SHARD, HV)


def solution(mesh):
    fine = Mesh(mesh.devices.reshape(NZ, NX, NC, NY), ("z", "x", "c", "y"))
    seq = ("z", "x", "c")
    in_specs = (P(("y",) + seq, None), P(None, seq)) + (P(),) * 9
    return jax.shard_map(
        per_device,
        mesh=fine,
        in_specs=in_specs,
        out_specs=P(("y",) + seq, None),
        check_vma=False,
    )
```

```python
import itertools

import jax
import jax.numpy as jnp
import numpy as np
from jax import lax
from jax.experimental import pallas as pl
from jax.experimental.pallas import tpu as pltpu
from jax.sharding import Mesh
from jax.sharding import PartitionSpec as P

H = 16
DK = 128
CONV = 4
D = 2304
HV = H * DK
BF = jnp.bfloat16
F32 = jnp.float32

NZ, NX, NC, NY = 4, 4, 2, 4
ROW = NX * NC
SHARD = 128
GROUP = ROW * SHARD
UNIT = 64
ROWS = D // 2
PACK = ROWS // 2
STEP = 2 * SHARD
VMEM_LIMIT = 56 * 1024 * 1024


def nearest(sources):
    def way(order):
        return sum(min((order[i] - sources[i] // ROW) % 4, (sources[i] // ROW - order[i]) % 4) for i in range(4))

    return min(itertools.permutations(range(4)), key=way)


def block_plan():
    whole_route, half_route, tables = [], [], []
    for group in range(ROW):
        blocks = [(kind, hp, 16 * kind + 2 * group + hp) for kind in range(3) for hp in range(2)]
        whole = [b for b in blocks if b[2] % 3 != 1]
        halves = [b for b in blocks if b[2] % 3 == 1]
        sources = [2 * (m // 3) + (m % 3) // 2 for _, _, m in whole]
        order = nearest(sources)
        at_z = [0] * 4
        for place, source, (kind, hp, _) in zip(order, sources, whole):
            whole_route.append((source, place * ROW + group))
            at_z[place] = 2 * kind + hp
        sources = [2 * (m // 3) + side for _, _, m in halves for side in range(2)]
        order = nearest(sources)
        for place, source in zip(order, sources):
            half_route.append((source, place * ROW + group))
        tables.append(at_z + [2 * kind + hp for kind, hp, _ in halves] + list(order))
    return sorted(whole_route), sorted(half_route), np.asarray(tables, np.int32)


WHOLE_ROUTE, HALF_ROUTE, TABLES = block_plan()


def ring(distance, size=4):
    return [(i, (i + distance) % size) for i in range(size)]


def ahead(distance, size=4):
    return [(i, i + distance) for i in range(size - distance)]


def split(x):
    high = x.astype(BF)
    return high, (x - high.astype(F32)).astype(BF)


def dot(a, b):
    return lax.dot_general(a, b, (((1,), (0,)), ((), ())), preferred_element_type=F32)


def dot_nt(a, b):
    return lax.dot_general(a, b, (((1,), (1,)), ((), ())), preferred_element_type=F32)


def mm3(a, b):
    ah, al = split(a)
    bh, bl = split(b)
    return dot(jnp.concatenate([ah, al, ah], axis=1), jnp.concatenate([bh, bh, bl], axis=0))


def mm3_nt(a, b):
    ah, al = split(a)
    bh, bl = split(b)
    return dot_nt(jnp.concatenate([ah, al, ah], axis=1), jnp.concatenate([bh, bh, bl], axis=1))


def sigmoid(x):
    return 1.0 / (1.0 + jnp.exp(-x))


def unit_lower_inverses(systems, rows, cols):
    eye = jnp.where(rows == cols, 1.0, 0.0)
    pair = (rows // 2) == (cols // 2)
    found = [eye - jnp.where(pair, a, 0.0) for a in systems]
    size = 2
    while size < SHARD:
        band = ((rows // (2 * size)) == (cols // (2 * size))) & ((rows // size) != (cols // size))
        low = [jnp.where(band, a, 0.0).astype(BF) for a in systems]
        near = [t.astype(BF) for t in found]
        half = [dot(t, a).astype(BF) for t, a in zip(near, low)]
        step = [dot(p, t) for p, t in zip(half, near)]
        found = [t - s for t, s in zip(found, step)]
        size *= 2
    near = [t.astype(BF) for t in found]
    parts = [jnp.concatenate(split(a), axis=1) for a in systems]
    rest = [
        eye - t.astype(F32) - dot(a, jnp.concatenate([t, t], axis=0)) for a, t in zip(parts, near)
    ]
    return [t.astype(F32) + dot(t, r.astype(BF)) for t, r in zip(near, rest)]


def fixed(shape):
    return pl.BlockSpec(shape, lambda i, s: (0,) * len(shape))


def by_group(shape, offset=0):
    return pl.BlockSpec(shape, lambda i, s: (0, s[2] + offset))


def by_step(columns):
    return pl.BlockSpec((STEP, columns), lambda i, s: (i, 0))


def block_columns(block):
    return pl.ds(pl.multiple_of(block * DK, DK), DK)


def fetch_weights(sp, parts, halves, weights, sems):
    z, mine = sp[0], lax.rem(sp[1], 2)
    copies = []
    for side in range(2):
        rows = mine if side == 0 else 1 - mine
        for k in range(NZ):
            part = parts[NZ * side + k]
            place = lax.rem(z - k + NZ, NZ)
            top = pl.multiple_of(rows * ROWS, 128)
            copies.append((part.at[pl.ds(0, ROWS)], weights.at[pl.ds(top, ROWS), block_columns(sp[3 + place])]))
            copies.append((part.at[pl.ds(ROWS, PACK)], halves.at[rows, place]))
    copies = [pltpu.make_async_copy(s, d, sems.at[i]) for i, (s, d) in enumerate(copies)]
    for copy in copies:
        copy.start()
    for copy in copies:
        copy.wait()
    for rows in range(2):
        for b in range(2):
            pair = [halves[rows, sp[9 + 2 * b + side]] for side in range(2)]
            cols = block_columns(sp[7 + b])
            weights[pl.ds(ROWS * rows, PACK), cols] = jnp.concatenate(
                [u[:, :UNIT] for u in pair], axis=1
            )
            weights[pl.ds(ROWS * rows + PACK, PACK), cols] = jnp.concatenate(
                [u[:, UNIT:] for u in pair], axis=1
            )


def params():
    return pltpu.CompilerParams(vmem_limit_bytes=VMEM_LIMIT)


def cost(flops, size):
    return pl.CostEstimate(flops=int(flops), bytes_accessed=int(size), transcendentals=0)


def gate_kernel(
    sp, tokens, wsmall, decay_up, gate_up, rate, scale, log_o, beta_o, gate_o
):
    g = sp[2]
    small = dot(tokens[...], wsmall[...])
    decay_low = small[:, :128].astype(BF)
    gate_low = small[:, 128:256].astype(BF)
    beta_all = scale[...] * sigmoid(small[:, 256:])
    logdec = -rate[...] * sigmoid(dot(decay_low, decay_up[...]))
    gate_o[...] = sigmoid(dot(gate_low, gate_up[...]))
    rows = lax.broadcasted_iota(jnp.int32, (SHARD, SHARD), 0)
    cols = lax.broadcasted_iota(jnp.int32, (SHARD, SHARD), 1)
    ones_low = jnp.where(rows >= cols, 1.0, 0.0).astype(BF)
    ones_twice = jnp.concatenate([ones_low, ones_low], axis=1)
    high, low = split(logdec)
    for blk in range(STEP // SHARD):
        ts = slice(SHARD * blk, SHARD * blk + SHARD)
        log_o[ts] = dot(ones_twice, jnp.concatenate([high[ts], low[ts]], axis=0))
    lane = lax.broadcasted_iota(jnp.int32, (STEP, 128), 1)
    for h in range(2):
        mine = jnp.sum(jnp.where(lane == 2 * g + h, beta_all, 0.0), axis=1, keepdims=True)
        beta_o[:, DK * h : DK * h + DK] = jnp.broadcast_to(mine, (STEP, DK))


def run_gates(sp, tokens, wsmall, decay_up, gate_up, rate, scale):
    wide = jax.ShapeDtypeStruct((GROUP, 2 * DK), F32)
    return pl.pallas_call(
        gate_kernel,
        name="block_gates",
        out_shape=(wide, wide, wide),
        grid_spec=pltpu.PrefetchScalarGridSpec(
            num_scalar_prefetch=1,
            grid=(GROUP // STEP,),
            in_specs=[
                by_step(D),
                fixed((D, 384)),
                by_group((128, 256)),
                by_group((128, 256)),
                by_group((1, 256)),
                fixed((1, 128)),
            ],
            out_specs=[by_step(2 * DK)] * 3,
        ),
        compiler_params=params(),
        cost_estimate=cost(2e9, 1e7),
    )(sp, tokens, wsmall, decay_up, gate_up, rate, scale)


def active(mixed, cols, taps):
    total = taps[0:1] * mixed[5 : 5 + STEP, cols]
    for j in range(1, CONV):
        total = total + taps[j : j + 1] * mixed[5 + j : 5 + j + STEP, cols]
    return total * sigmoid(total)


def state_kernel(sp, tokens, halo, log_sums, betas, conv_k, conv_v, *rest):
    parts = rest[:8]
    down_o, solved_o, carry_o, wq_o, state_o = rest[8:13]
    halves, wbuf, mixed, state, sems = rest[13:]
    step = pl.program_id(0)

    @pl.when(step == 0)
    def _():
        fetch_weights(sp, parts, halves, wbuf, sems)
        wq_o[...] = wbuf[:, : 2 * DK]
        before = dot(halo[...], wbuf[:, 2 * DK :]).astype(BF).astype(F32)
        mixed[0:8] = before[8:16]
        rr = lax.broadcasted_iota(jnp.int32, (DK, 2 * DK), 0)
        cc = lax.broadcasted_iota(jnp.int32, (DK, 2 * DK), 1)
        start = jnp.where(rr == cc, 1.0, 0.0)
        state[0] = start
        state[1] = start

    mixed[8:] = dot(tokens[...], wbuf[:, 2 * DK :]).astype(BF).astype(F32)
    keys = active(mixed, slice(0, 256), conv_k)
    values = active(mixed, slice(256, 512), conv_v)
    mixed[0:8] = mixed[STEP : STEP + 8]

    rows = lax.broadcasted_iota(jnp.int32, (SHARD, SHARD), 0)
    cols = lax.broadcasted_iota(jnp.int32, (SHARD, SHARD), 1)
    places = [
        (h, blk, slice(SHARD * blk, SHARD * blk + SHARD), slice(DK * h, DK * h + DK))
        for blk in range(STEP // SHARD)
        for h in range(2)
    ]
    systems, sides, ends, tails = [], [], [], []
    for h, blk, ts, hs in places:
        k, beta, log_sum = keys[ts, hs], betas[ts, hs], log_sums[ts, hs]
        k = k * lax.rsqrt(jnp.sum(k * k, axis=1, keepdims=True) + 1e-06)
        end = log_sum[SHARD - 1 : SHARD]
        k_up = k * jnp.exp(log_sum)
        k_down = k * jnp.exp(-log_sum)
        down_o[ts, hs] = k_down
        systems.append(jnp.where(rows > cols, mm3_nt(k_up, k_down), 0.0) * beta)
        sides.append(jnp.concatenate([k_up * beta, values[ts, hs] * beta], axis=1))
        ends.append((k * jnp.exp(end - log_sum)).T)
        tails.append(jnp.where(rows == cols, jnp.exp(end), 0.0))
    inverses = unit_lower_inverses(systems, rows, cols)
    solved = [mm3(t, r) for t, r in zip(inverses, sides)]
    moves = [mm3(e, s) for e, s in zip(ends, solved)]
    for (h, blk, ts, hs), tail, sol, move in zip(places, tails, solved, moves):
        solved_o[ts, 2 * DK * h : 2 * DK * h + 2 * DK] = sol
        carry = state[h]
        carry_o[ts, 2 * DK * h : 2 * DK * h + 2 * DK] = carry
        new = mm3(tail - move[:, :DK], carry)
        state[h, :, :DK] = new[:, :DK]
        state[h, :, DK:] = new[:, DK:] + move[:, DK:]

    @pl.when(step == pl.num_programs(0) - 1)
    def _():
        state_o[...] = state[...]


def run_state(sp, tokens, halo, log_sums, betas, conv, parts):
    return pl.pallas_call(
        state_kernel,
        name="block_state",
        out_shape=(
            jax.ShapeDtypeStruct((GROUP, 2 * DK), F32),
            jax.ShapeDtypeStruct((GROUP, 4 * DK), F32),
            jax.ShapeDtypeStruct((GROUP, 4 * DK), F32),
            jax.ShapeDtypeStruct((D, 2 * DK), BF),
            jax.ShapeDtypeStruct((2, DK, 2 * DK), F32),
        ),
        grid_spec=pltpu.PrefetchScalarGridSpec(
            num_scalar_prefetch=1,
            grid=(GROUP // STEP,),
            in_specs=[
                by_step(D),
                fixed((16, D)),
                by_step(2 * DK),
                by_step(2 * DK),
                by_group((CONV, 256), 8),
                by_group((CONV, 256), 16),
            ]
            + [pl.BlockSpec(memory_space=pl.ANY)] * 8,
            out_specs=[
                by_step(2 * DK),
                by_step(4 * DK),
                by_step(4 * DK),
                fixed((D, 2 * DK)),
                fixed((2, DK, 2 * DK)),
            ],
            scratch_shapes=[
                pltpu.VMEM((2, NZ, PACK, 128), BF),
                pltpu.VMEM((D, 6 * DK), BF),
                pltpu.VMEM((8 + STEP, 512), F32),
                pltpu.VMEM((2, DK, 2 * DK), F32),
                pltpu.SemaphoreType.DMA((16,)),
            ],
        ),
        compiler_params=params(),
        cost_estimate=cost(1e10, 2e7),
    )(sp, tokens, halo, log_sums, betas, conv, conv, *parts)


def query_kernel(
    sp, tokens, halo, wq, conv_q, log_sums, k_downs, solved, carries, qeff_o, core_o, mixed
):
    @pl.when(pl.program_id(0) == 0)
    def _():
        before = dot(halo[...], wq[...]).astype(BF).astype(F32)
        mixed[0:8] = before[8:16]

    mixed[8:] = dot(tokens[...], wq[...]).astype(BF).astype(F32)
    query = active(mixed, slice(0, 256), conv_q)
    mixed[0:8] = mixed[STEP : STEP + 8]
    rows = lax.broadcasted_iota(jnp.int32, (SHARD, SHARD), 0)
    cols = lax.broadcasted_iota(jnp.int32, (SHARD, SHARD), 1)
    for blk in range(STEP // SHARD):
        for h in range(2):
            ts = slice(SHARD * blk, SHARD * blk + SHARD)
            hs = slice(DK * h, DK * h + DK)
            both = slice(2 * DK * h, 2 * DK * h + 2 * DK)
            q = query[ts, hs]
            q = q * (lax.rsqrt(jnp.sum(q * q, axis=1, keepdims=True) + 1e-06) * DK**-0.5)
            q_up = q * jnp.exp(log_sums[ts, hs])
            attend = jnp.where(rows >= cols, mm3_nt(q_up, k_downs[ts, hs]), 0.0)
            within = mm3(attend, solved[ts, both])
            out = mm3(q_up - within[:, :DK], carries[ts, both])
            qeff_o[ts, hs] = out[:, :DK]
            core_o[ts, hs] = out[:, DK:] + within[:, DK:]


def run_queries(sp, tokens, halo, wq, conv, log_sums, k_downs, solved, carries):
    wide = jax.ShapeDtypeStruct((GROUP, 2 * DK), F32)
    return pl.pallas_call(
        query_kernel,
        name="block_query",
        out_shape=(wide, wide),
        grid_spec=pltpu.PrefetchScalarGridSpec(
            num_scalar_prefetch=1,
            grid=(GROUP // STEP,),
            in_specs=[
                by_step(D),
                fixed((16, D)),
                fixed((D, 2 * DK)),
                by_group((CONV, 256)),
                by_step(2 * DK),
                by_step(2 * DK),
                by_step(4 * DK),
                by_step(4 * DK),
            ],
            out_specs=[by_step(2 * DK)] * 2,
            scratch_shapes=[pltpu.VMEM((8 + STEP, 256), F32)],
        ),
        compiler_params=params(),
        cost_estimate=cost(5e9, 2e7),
    )(sp, tokens, halo, wq, conv, log_sums, k_downs, solved, carries)


def finish_kernel(near, middle, far, qeff, core, gate, gain, out, state):
    @pl.when(pl.program_id(0) == 0)
    def _():
        for h in range(2):
            carry = middle[h, :, DK:] + mm3(middle[h, :, :DK], far[h])
            state[h] = near[h, :, DK:] + mm3(near[h, :, :DK], carry)

    for h in range(2):
        hs = slice(DK * h, DK * h + DK)
        full = core[:, hs] + mm3(qeff[:, hs], state[h])
        scale = lax.rsqrt(jnp.mean(full * full, axis=1, keepdims=True) + 1e-06)
        out[:, hs] = (full * scale * gain[...] * gate[:, hs]).astype(BF)


def run_finish(near, middle, far, qeff, core, gate, gain):
    def whole(shape):
        return pl.BlockSpec(shape, lambda i: (0,) * len(shape))

    tile = pl.BlockSpec((256, 2 * DK), lambda i: (i, 0))
    return pl.pallas_call(
        finish_kernel,
        name="finish",
        out_shape=jax.ShapeDtypeStruct((GROUP, 2 * DK), BF),
        grid=(GROUP // 256,),
        in_specs=[
            whole((2, DK, 2 * DK)),
            whole((2, DK, 2 * DK)),
            whole((2, DK, DK)),
            tile,
            tile,
            tile,
            whole((1, DK)),
        ],
        out_specs=tile,
        scratch_shapes=[pltpu.VMEM((2, DK, DK), F32)],
        compiler_params=pltpu.CompilerParams(vmem_limit_bytes=VMEM_LIMIT),
    )(near, middle, far, qeff, core, gate, gain)


def gather_weights(weight, c, y):
    rows = lax.dynamic_slice(weight, (ROWS * lax.rem(y, 2), 0), (ROWS, 3 * UNIT))
    whole = jnp.where(c == 0, rows[:, : 2 * UNIT], rows[:, UNIT:])
    half = jnp.where(c == 0, rows[:, 2 * UNIT :], rows[:, :UNIT])
    half = jnp.concatenate([half[:PACK], half[PACK:]], axis=1)
    seq = ("z", "x", "c")
    mine = jnp.concatenate(
        [lax.ppermute(whole, seq, WHOLE_ROUTE), lax.ppermute(half, seq, HALF_ROUTE)], axis=0
    )
    near = [mine] + [lax.ppermute(mine, "z", ring(k)) for k in range(1, NZ)]
    return near, [lax.ppermute(p, "y", ring(d)) for p, d in zip(near, (1, 3, 3, 1))]


def per_device(
    tokens,
    qkv_weight,
    conv_weight,
    decay_down,
    decay_up,
    decay_rate,
    beta_weight,
    beta_scale,
    gate_down,
    gate_up,
    norm_gain,
):
    z, x, c, y = (lax.axis_index(a) for a in ("z", "x", "c", "y"))
    g = x * NC + c
    wsmall = jnp.concatenate(
        [decay_down, gate_down, jnp.pad(beta_weight, ((0, 0), (0, 128 - H)))], axis=1
    )
    sp = jnp.concatenate([jnp.stack([z, y, g]).astype(jnp.int32), jnp.asarray(TABLES)[g]])
    scale = jnp.pad(beta_scale, (0, 128 - H)).reshape(1, 128)
    row = lax.all_gather(tokens, ("x", "c"), axis=0, tiled=True)
    near, far = gather_weights(qkv_weight, c, y)
    halo = lax.ppermute(row[GROUP - 16 :], "z", ahead(1))
    log_sums, betas, gate = run_gates(
        sp,
        row,
        wsmall,
        decay_up,
        gate_up,
        decay_rate.reshape(1, HV),
        scale,
    )
    k_downs, solved, carries, wq, state = run_state(
        sp, row, halo, log_sums, betas, conv_weight, near + far
    )
    first = lax.ppermute(state, "z", ahead(1))
    second = lax.ppermute(state, "z", ahead(2))
    third = lax.ppermute(state[:, :, DK:], "z", ahead(3))
    qeff, core = run_queries(sp, row, halo, wq, conv_weight, log_sums, k_downs, solved, carries)
    out = run_finish(first, second, third, qeff, core, gate, norm_gain.reshape(1, DK))
    out = lax.all_to_all(out.reshape(ROW, SHARD, 2 * DK), ("x", "c"), 0, 0)
    return out.transpose(1, 0, 2).reshape(SHARD, HV)


def solution(mesh):
    fine = Mesh(mesh.devices.reshape(NZ, NX, NC, NY), ("z", "x", "c", "y"))
    seq = ("z", "x", "c")
    in_specs = (P(("y",) + seq, None), P(None, seq)) + (P(),) * 9
    return jax.shard_map(
        per_device,
        mesh=fine,
        in_specs=in_specs,
        out_specs=P(("y",) + seq, None),
        check_vma=False,
    )
```

```python
import itertools

import jax
import jax.numpy as jnp
import numpy as np
from jax import lax
from jax.experimental import pallas as pl
from jax.experimental.pallas import tpu as pltpu
from jax.sharding import Mesh
from jax.sharding import PartitionSpec as P

H = 16
DK = 128
CONV = 4
D = 2304
HV = H * DK
BF = jnp.bfloat16
F32 = jnp.float32

NZ, NX, NC, NY = 4, 4, 2, 4
ROW = NX * NC
SHARD = 128
GROUP = ROW * SHARD
UNIT = 64
ROWS = D // 2
PACK = ROWS // 2
STEP = 4 * SHARD
VMEM_LIMIT = 56 * 1024 * 1024


def nearest(sources):
    def way(order):
        return sum(min((order[i] - sources[i] // ROW) % 4, (sources[i] // ROW - order[i]) % 4) for i in range(4))

    return min(itertools.permutations(range(4)), key=way)


def block_plan():
    whole_route, half_route, tables = [], [], []
    for group in range(ROW):
        blocks = [(kind, hp, 16 * kind + 2 * group + hp) for kind in range(3) for hp in range(2)]
        whole = [b for b in blocks if b[2] % 3 != 1]
        halves = [b for b in blocks if b[2] % 3 == 1]
        sources = [2 * (m // 3) + (m % 3) // 2 for _, _, m in whole]
        order = nearest(sources)
        at_z = [0] * 4
        for place, source, (kind, hp, _) in zip(order, sources, whole):
            whole_route.append((source, place * ROW + group))
            at_z[place] = 2 * kind + hp
        sources = [2 * (m // 3) + side for _, _, m in halves for side in range(2)]
        order = nearest(sources)
        for place, source in zip(order, sources):
            half_route.append((source, place * ROW + group))
        tables.append(at_z + [2 * kind + hp for kind, hp, _ in halves] + list(order))
    return sorted(whole_route), sorted(half_route), np.asarray(tables, np.int32)


WHOLE_ROUTE, HALF_ROUTE, TABLES = block_plan()


def ring(distance, size=4):
    return [(i, (i + distance) % size) for i in range(size)]


def ahead(distance, size=4):
    return [(i, i + distance) for i in range(size - distance)]


def split(x):
    high = x.astype(BF)
    return high, (x - high.astype(F32)).astype(BF)


def dot(a, b):
    return lax.dot_general(a, b, (((1,), (0,)), ((), ())), preferred_element_type=F32)


def dot_nt(a, b):
    return lax.dot_general(a, b, (((1,), (1,)), ((), ())), preferred_element_type=F32)


def mm3(a, b):
    ah, al = split(a)
    bh, bl = split(b)
    return dot(jnp.concatenate([ah, al, ah], axis=1), jnp.concatenate([bh, bh, bl], axis=0))


def mm3_nt(a, b):
    ah, al = split(a)
    bh, bl = split(b)
    return dot_nt(jnp.concatenate([ah, al, ah], axis=1), jnp.concatenate([bh, bh, bl], axis=1))


def sigmoid(x):
    return 1.0 / (1.0 + jnp.exp(-x))


def unit_lower_inverses(systems, rows, cols):
    eye = jnp.where(rows == cols, 1.0, 0.0)
    pair = (rows // 2) == (cols // 2)
    found = [eye - jnp.where(pair, a, 0.0) for a in systems]
    size = 2
    while size < SHARD:
        band = ((rows // (2 * size)) == (cols // (2 * size))) & ((rows // size) != (cols // size))
        low = [jnp.where(band, a, 0.0).astype(BF) for a in systems]
        near = [t.astype(BF) for t in found]
        half = [dot(t, a).astype(BF) for t, a in zip(near, low)]
        step = [dot(p, t) for p, t in zip(half, near)]
        found = [t - s for t, s in zip(found, step)]
        size *= 2
    near = [t.astype(BF) for t in found]
    parts = [jnp.concatenate(split(a), axis=1) for a in systems]
    rest = [
        eye - t.astype(F32) - dot(a, jnp.concatenate([t, t], axis=0)) for a, t in zip(parts, near)
    ]
    return [t.astype(F32) + dot(t, r.astype(BF)) for t, r in zip(near, rest)]


def fixed(shape):
    return pl.BlockSpec(shape, lambda i, s: (0,) * len(shape))


def by_group(shape, offset=0):
    return pl.BlockSpec(shape, lambda i, s: (0, s[2] + offset))


def by_step(columns):
    return pl.BlockSpec((STEP, columns), lambda i, s: (i, 0))


def block_columns(block):
    return pl.ds(pl.multiple_of(block * DK, DK), DK)


def fetch_weights(sp, parts, halves, weights, sems):
    z, mine = sp[0], lax.rem(sp[1], 2)
    copies = []
    for side in range(2):
        rows = mine if side == 0 else 1 - mine
        for k in range(NZ):
            part = parts[NZ * side + k]
            place = lax.rem(z - k + NZ, NZ)
            top = pl.multiple_of(rows * ROWS, 128)
            copies.append((part.at[pl.ds(0, ROWS)], weights.at[pl.ds(top, ROWS), block_columns(sp[3 + place])]))
            copies.append((part.at[pl.ds(ROWS, PACK)], halves.at[rows, place]))
    copies = [pltpu.make_async_copy(s, d, sems.at[i]) for i, (s, d) in enumerate(copies)]
    for copy in copies:
        copy.start()
    for copy in copies:
        copy.wait()
    for rows in range(2):
        for b in range(2):
            pair = [halves[rows, sp[9 + 2 * b + side]] for side in range(2)]
            cols = block_columns(sp[7 + b])
            weights[pl.ds(ROWS * rows, PACK), cols] = jnp.concatenate(
                [u[:, :UNIT] for u in pair], axis=1
            )
            weights[pl.ds(ROWS * rows + PACK, PACK), cols] = jnp.concatenate(
                [u[:, UNIT:] for u in pair], axis=1
            )


def params():
    return pltpu.CompilerParams(vmem_limit_bytes=VMEM_LIMIT)


def cost(flops, size):
    return pl.CostEstimate(flops=int(flops), bytes_accessed=int(size), transcendentals=0)


def gate_kernel(
    sp, tokens, wsmall, decay_up, gate_up, rate, scale, log_o, beta_o, gate_o
):
    g = sp[2]
    small = dot(tokens[...], wsmall[...])
    decay_low = small[:, :128].astype(BF)
    gate_low = small[:, 128:256].astype(BF)
    beta_all = scale[...] * sigmoid(small[:, 256:])
    logdec = -rate[...] * sigmoid(dot(decay_low, decay_up[...]))
    gate_o[...] = sigmoid(dot(gate_low, gate_up[...]))
    rows = lax.broadcasted_iota(jnp.int32, (SHARD, SHARD), 0)
    cols = lax.broadcasted_iota(jnp.int32, (SHARD, SHARD), 1)
    ones_low = jnp.where(rows >= cols, 1.0, 0.0).astype(BF)
    ones_twice = jnp.concatenate([ones_low, ones_low], axis=1)
    high, low = split(logdec)
    for blk in range(STEP // SHARD):
        ts = slice(SHARD * blk, SHARD * blk + SHARD)
        log_o[ts] = dot(ones_twice, jnp.concatenate([high[ts], low[ts]], axis=0))
    lane = lax.broadcasted_iota(jnp.int32, (STEP, 128), 1)
    for h in range(2):
        mine = jnp.sum(jnp.where(lane == 2 * g + h, beta_all, 0.0), axis=1, keepdims=True)
        beta_o[:, DK * h : DK * h + DK] = jnp.broadcast_to(mine, (STEP, DK))


def run_gates(sp, tokens, wsmall, decay_up, gate_up, rate, scale):
    wide = jax.ShapeDtypeStruct((GROUP, 2 * DK), F32)
    return pl.pallas_call(
        gate_kernel,
        name="block_gates",
        out_shape=(wide, wide, wide),
        grid_spec=pltpu.PrefetchScalarGridSpec(
            num_scalar_prefetch=1,
            grid=(GROUP // STEP,),
            in_specs=[
                by_step(D),
                fixed((D, 384)),
                by_group((128, 256)),
                by_group((128, 256)),
                by_group((1, 256)),
                fixed((1, 128)),
            ],
            out_specs=[by_step(2 * DK)] * 3,
        ),
        compiler_params=params(),
        cost_estimate=cost(2e9, 1e7),
    )(sp, tokens, wsmall, decay_up, gate_up, rate, scale)


def active(mixed, cols, taps):
    total = taps[0:1] * mixed[5 : 5 + STEP, cols]
    for j in range(1, CONV):
        total = total + taps[j : j + 1] * mixed[5 + j : 5 + j + STEP, cols]
    return total * sigmoid(total)


def state_kernel(sp, tokens, halo, log_sums, betas, conv_k, conv_v, *rest):
    parts = rest[:8]
    down_o, solved_o, carry_o, wq_o, state_o, offset_o = rest[8:14]
    halves, wbuf, mixed, state, sems = rest[14:]
    step = pl.program_id(0)

    @pl.when(step == 0)
    def _():
        fetch_weights(sp, parts, halves, wbuf, sems)
        wq_o[...] = wbuf[:, : 2 * DK]
        before = dot(halo[...], wbuf[:, 2 * DK :]).astype(BF).astype(F32)
        mixed[0:8] = before[8:16]
        rr = lax.broadcasted_iota(jnp.int32, (DK, 2 * DK), 0)
        cc = lax.broadcasted_iota(jnp.int32, (DK, 2 * DK), 1)
        start = jnp.where(rr == cc, 1.0, 0.0)
        state[0] = start
        state[1] = start

    mixed[8:] = dot(tokens[...], wbuf[:, 2 * DK :]).astype(BF).astype(F32)
    keys = active(mixed, slice(0, 256), conv_k)
    values = active(mixed, slice(256, 512), conv_v)
    mixed[0:8] = mixed[STEP : STEP + 8]

    rows = lax.broadcasted_iota(jnp.int32, (SHARD, SHARD), 0)
    cols = lax.broadcasted_iota(jnp.int32, (SHARD, SHARD), 1)
    places = [
        (h, blk, slice(SHARD * blk, SHARD * blk + SHARD), slice(DK * h, DK * h + DK))
        for blk in range(STEP // SHARD)
        for h in range(2)
    ]
    systems, sides, ends, tails = [], [], [], []
    for h, blk, ts, hs in places:
        k, beta, log_sum = keys[ts, hs], betas[ts, hs], log_sums[ts, hs]
        k = k * lax.rsqrt(jnp.sum(k * k, axis=1, keepdims=True) + 1e-06)
        end = log_sum[SHARD - 1 : SHARD]
        k_up = k * jnp.exp(log_sum)
        k_down = k * jnp.exp(-log_sum)
        down_o[ts, hs] = k_down
        systems.append(jnp.where(rows > cols, mm3_nt(k_up, k_down), 0.0) * beta)
        sides.append(jnp.concatenate([k_up * beta, values[ts, hs] * beta], axis=1))
        ends.append((k * jnp.exp(end - log_sum)).T)
        tails.append(jnp.where(rows == cols, jnp.exp(end), 0.0))
    inverses = unit_lower_inverses(systems, rows, cols)
    solved = [mm3(t, r) for t, r in zip(inverses, sides)]
    moves = [mm3(e, s) for e, s in zip(ends, solved)]
    for (h, blk, ts, hs), tail, sol, move in zip(places, tails, solved, moves):
        solved_o[ts, 2 * DK * h : 2 * DK * h + 2 * DK] = sol
        carry = state[h]
        carry_o[ts, 2 * DK * h : 2 * DK * h + 2 * DK] = carry
        new = mm3(tail - move[:, :DK], carry)
        state[h, :, :DK] = new[:, :DK]
        state[h, :, DK:] = new[:, DK:] + move[:, DK:]

    @pl.when(step == pl.num_programs(0) - 1)
    def _():
        state_o[...] = state[...]
        offset_o[...] = state[:, :, DK:]


def run_state(sp, tokens, halo, log_sums, betas, conv, parts):
    return pl.pallas_call(
        state_kernel,
        name="block_state",
        out_shape=(
            jax.ShapeDtypeStruct((GROUP, 2 * DK), F32),
            jax.ShapeDtypeStruct((GROUP, 4 * DK), F32),
            jax.ShapeDtypeStruct((GROUP, 4 * DK), F32),
            jax.ShapeDtypeStruct((D, 2 * DK), BF),
            jax.ShapeDtypeStruct((2, DK, 2 * DK), F32),
            jax.ShapeDtypeStruct((2, DK, DK), F32),
        ),
        grid_spec=pltpu.PrefetchScalarGridSpec(
            num_scalar_prefetch=1,
            grid=(GROUP // STEP,),
            in_specs=[
                by_step(D),
                fixed((16, D)),
                by_step(2 * DK),
                by_step(2 * DK),
                by_group((CONV, 256), 8),
                by_group((CONV, 256), 16),
            ]
            + [pl.BlockSpec(memory_space=pl.ANY)] * 8,
            out_specs=[
                by_step(2 * DK),
                by_step(4 * DK),
                by_step(4 * DK),
                fixed((D, 2 * DK)),
                fixed((2, DK, 2 * DK)),
                fixed((2, DK, DK)),
            ],
            scratch_shapes=[
                pltpu.VMEM((2, NZ, PACK, 128), BF),
                pltpu.VMEM((D, 6 * DK), BF),
                pltpu.VMEM((8 + STEP, 512), F32),
                pltpu.VMEM((2, DK, 2 * DK), F32),
                pltpu.SemaphoreType.DMA((16,)),
            ],
        ),
        compiler_params=params(),
        cost_estimate=cost(1e10, 2e7),
    )(sp, tokens, halo, log_sums, betas, conv, conv, *parts)


def query_kernel(
    sp, tokens, halo, wq, conv_q, log_sums, k_downs, solved, carries, qeff_o, core_o, mixed
):
    @pl.when(pl.program_id(0) == 0)
    def _():
        before = dot(halo[...], wq[...]).astype(BF).astype(F32)
        mixed[0:8] = before[8:16]

    mixed[8:] = dot(tokens[...], wq[...]).astype(BF).astype(F32)
    query = active(mixed, slice(0, 256), conv_q)
    mixed[0:8] = mixed[STEP : STEP + 8]
    rows = lax.broadcasted_iota(jnp.int32, (SHARD, SHARD), 0)
    cols = lax.broadcasted_iota(jnp.int32, (SHARD, SHARD), 1)
    places = [
        (
            slice(SHARD * blk, SHARD * blk + SHARD),
            slice(DK * h, DK * h + DK),
            slice(2 * DK * h, 2 * DK * h + 2 * DK),
        )
        for blk in range(STEP // SHARD)
        for h in range(2)
    ]
    ups = []
    for ts, hs, _ in places:
        q = query[ts, hs]
        q = q * (lax.rsqrt(jnp.sum(q * q, axis=1, keepdims=True) + 1e-06) * DK**-0.5)
        ups.append(q * jnp.exp(log_sums[ts, hs]))
    scores = [mm3_nt(u, k_downs[ts, hs]) for u, (ts, hs, _) in zip(ups, places)]
    attends = [jnp.where(rows >= cols, a, 0.0) for a in scores]
    withins = [mm3(a, solved[ts, both]) for a, (ts, _, both) in zip(attends, places)]
    outs = [
        mm3(u - w[:, :DK], carries[ts, both]) for u, w, (ts, _, both) in zip(ups, withins, places)
    ]
    for out, w, (ts, hs, _) in zip(outs, withins, places):
        qeff_o[ts, hs] = out[:, :DK]
        core_o[ts, hs] = out[:, DK:] + w[:, DK:]


def run_queries(sp, tokens, halo, wq, conv, log_sums, k_downs, solved, carries):
    wide = jax.ShapeDtypeStruct((GROUP, 2 * DK), F32)
    return pl.pallas_call(
        query_kernel,
        name="block_query",
        out_shape=(wide, wide),
        grid_spec=pltpu.PrefetchScalarGridSpec(
            num_scalar_prefetch=1,
            grid=(GROUP // STEP,),
            in_specs=[
                by_step(D),
                fixed((16, D)),
                fixed((D, 2 * DK)),
                by_group((CONV, 256)),
                by_step(2 * DK),
                by_step(2 * DK),
                by_step(4 * DK),
                by_step(4 * DK),
            ],
            out_specs=[by_step(2 * DK)] * 2,
            scratch_shapes=[pltpu.VMEM((8 + STEP, 256), F32)],
        ),
        compiler_params=params(),
        cost_estimate=cost(5e9, 2e7),
    )(sp, tokens, halo, wq, conv, log_sums, k_downs, solved, carries)


def finish_kernel(near, middle, far, qeff, core, gate, gain, out, state):
    heads = range(2)

    @pl.when(pl.program_id(0) == 0)
    def _():
        carries = [middle[h, :, DK:] + mm3(middle[h, :, :DK], far[h]) for h in heads]
        starts = [near[h, :, DK:] + mm3(near[h, :, :DK], carries[h]) for h in heads]
        for h in heads:
            state[h] = starts[h]

    spans = [slice(DK * h, DK * h + DK) for h in heads]
    added = [mm3(qeff[:, hs], state[h]) for h, hs in zip(heads, spans)]
    for hs, more in zip(spans, added):
        full = core[:, hs] + more
        scale = lax.rsqrt(jnp.mean(full * full, axis=1, keepdims=True) + 1e-06)
        out[:, hs] = (full * scale * gain[...] * gate[:, hs]).astype(BF)


def run_finish(near, middle, far, qeff, core, gate, gain):
    def whole(shape):
        return pl.BlockSpec(shape, lambda i: (0,) * len(shape))

    tile = pl.BlockSpec((512, 2 * DK), lambda i: (i, 0))
    return pl.pallas_call(
        finish_kernel,
        name="finish",
        out_shape=jax.ShapeDtypeStruct((GROUP, 2 * DK), BF),
        grid=(GROUP // 512,),
        in_specs=[
            whole((2, DK, 2 * DK)),
            whole((2, DK, 2 * DK)),
            whole((2, DK, DK)),
            tile,
            tile,
            tile,
            whole((1, DK)),
        ],
        out_specs=tile,
        scratch_shapes=[pltpu.VMEM((2, DK, DK), F32)],
        compiler_params=pltpu.CompilerParams(vmem_limit_bytes=VMEM_LIMIT),
    )(near, middle, far, qeff, core, gate, gain)


def gather_weights(weight, c, y):
    rows = lax.dynamic_slice(weight, (ROWS * lax.rem(y, 2), 0), (ROWS, 3 * UNIT))
    whole = jnp.where(c == 0, rows[:, : 2 * UNIT], rows[:, UNIT:])
    half = jnp.where(c == 0, rows[:, 2 * UNIT :], rows[:, :UNIT])
    half = jnp.concatenate([half[:PACK], half[PACK:]], axis=1)
    seq = ("z", "x", "c")
    mine = jnp.concatenate(
        [lax.ppermute(whole, seq, WHOLE_ROUTE), lax.ppermute(half, seq, HALF_ROUTE)], axis=0
    )
    near = [mine] + [lax.ppermute(mine, "z", ring(k)) for k in range(1, NZ)]
    return near, [lax.ppermute(p, "y", ring(d)) for p, d in zip(near, (1, 3, 3, 1))]


def per_device(
    tokens,
    qkv_weight,
    conv_weight,
    decay_down,
    decay_up,
    decay_rate,
    beta_weight,
    beta_scale,
    gate_down,
    gate_up,
    norm_gain,
):
    z, x, c, y = (lax.axis_index(a) for a in ("z", "x", "c", "y"))
    g = x * NC + c
    wsmall = jnp.concatenate(
        [decay_down, gate_down, jnp.pad(beta_weight, ((0, 0), (0, 128 - H)))], axis=1
    )
    sp = jnp.concatenate([jnp.stack([z, y, g]).astype(jnp.int32), jnp.asarray(TABLES)[g]])
    scale = jnp.pad(beta_scale, (0, 128 - H)).reshape(1, 128)
    row = lax.all_gather(tokens, ("x", "c"), axis=0, tiled=True)
    near, far = gather_weights(qkv_weight, c, y)
    halo = lax.ppermute(row[GROUP - 16 :], "z", ahead(1))
    log_sums, betas, gate = run_gates(
        sp,
        row,
        wsmall,
        decay_up,
        gate_up,
        decay_rate.reshape(1, HV),
        scale,
    )
    k_downs, solved, carries, wq, state, offset = run_state(
        sp, row, halo, log_sums, betas, conv_weight, near + far
    )
    first = lax.ppermute(state, "z", ahead(1))
    second = lax.ppermute(state, "z", ahead(2))
    third = lax.ppermute(offset, "z", ahead(3))
    qeff, core = run_queries(sp, row, halo, wq, conv_weight, log_sums, k_downs, solved, carries)
    out = run_finish(first, second, third, qeff, core, gate, norm_gain.reshape(1, DK))
    out = lax.all_to_all(out.reshape(ROW, SHARD, 2 * DK), ("x", "c"), 0, 0)
    return out.transpose(1, 0, 2).reshape(SHARD, HV)


def solution(mesh):
    fine = Mesh(mesh.devices.reshape(NZ, NX, NC, NY), ("z", "x", "c", "y"))
    seq = ("z", "x", "c")
    in_specs = (P(("y",) + seq, None), P(None, seq)) + (P(),) * 9
    return jax.shard_map(
        per_device,
        mesh=fine,
        in_specs=in_specs,
        out_specs=P(("y",) + seq, None),
        check_vma=False,
    )
```

```python
import itertools

import jax
import jax.numpy as jnp
import numpy as np
from jax import lax
from jax.experimental import pallas as pl
from jax.experimental.pallas import tpu as pltpu
from jax.sharding import Mesh
from jax.sharding import PartitionSpec as P

H = 16
DK = 128
CONV = 4
D = 2304
HV = H * DK
BF = jnp.bfloat16
F32 = jnp.float32

NZ, NX, NC, NY = 4, 4, 2, 4
ROW = NX * NC
SHARD = 128
GROUP = ROW * SHARD
UNIT = 64
ROWS = D // 2
PACK = ROWS // 2
STEP = 4 * SHARD
VMEM_LIMIT = 56 * 1024 * 1024


def nearest(sources):
    def way(order):
        return sum(min((order[i] - sources[i] // ROW) % 4, (sources[i] // ROW - order[i]) % 4) for i in range(4))

    return min(itertools.permutations(range(4)), key=way)


def first_head(x, c):
    return (x ^ 1) + 8 * c


def block_plan():
    whole_route, half_route, tables = [], [], []
    for group in range(ROW):
        head = first_head(group // NC, group % NC)
        blocks = [(kind, hp, 16 * kind + head + 4 * hp) for kind in range(3) for hp in range(2)]
        whole = [b for b in blocks if b[2] % 3 != 1]
        halves = [b for b in blocks if b[2] % 3 == 1]
        sources = [2 * (m // 3) + (m % 3) // 2 for _, _, m in whole]
        order = nearest(sources)
        at_z = [0] * 4
        for place, source, (kind, hp, _) in zip(order, sources, whole):
            whole_route.append((source, place * ROW + group))
            at_z[place] = 2 * kind + hp
        sources = [2 * (m // 3) + side for _, _, m in halves for side in range(2)]
        order = nearest(sources)
        for place, source in zip(order, sources):
            half_route.append((source, place * ROW + group))
        tables.append(at_z + [2 * kind + hp for kind, hp, _ in halves] + list(order))
    return sorted(whole_route), sorted(half_route), np.asarray(tables, np.int32)


WHOLE_ROUTE, HALF_ROUTE, TABLES = block_plan()


def ring(distance, size=4):
    return [(i, (i + distance) % size) for i in range(size)]


def ahead(distance, size=4):
    return [(i, i + distance) for i in range(size - distance)]


def split(x):
    high = x.astype(BF)
    return high, (x - high.astype(F32)).astype(BF)


def dot(a, b):
    return lax.dot_general(a, b, (((1,), (0,)), ((), ())), preferred_element_type=F32)


def dot_nt(a, b):
    return lax.dot_general(a, b, (((1,), (1,)), ((), ())), preferred_element_type=F32)


def mm3(a, b):
    ah, al = split(a)
    bh, bl = split(b)
    return dot(jnp.concatenate([ah, al, ah], axis=1), jnp.concatenate([bh, bh, bl], axis=0))


def mm3_nt(a, b):
    ah, al = split(a)
    bh, bl = split(b)
    return dot_nt(jnp.concatenate([ah, al, ah], axis=1), jnp.concatenate([bh, bh, bl], axis=1))


def sigmoid(x):
    return 1.0 / (1.0 + jnp.exp(-x))


def unit_lower_inverses(systems, rows, cols):
    eye = jnp.where(rows == cols, 1.0, 0.0)
    pair = (rows // 2) == (cols // 2)
    found = [eye - jnp.where(pair, a, 0.0) for a in systems]
    size = 2
    while size < SHARD:
        band = ((rows // (2 * size)) == (cols // (2 * size))) & ((rows // size) != (cols // size))
        low = [jnp.where(band, a, 0.0).astype(BF) for a in systems]
        near = [t.astype(BF) for t in found]
        half = [dot(t, a).astype(BF) for t, a in zip(near, low)]
        step = [dot(p, t) for p, t in zip(half, near)]
        found = [t - s for t, s in zip(found, step)]
        size *= 2
    near = [t.astype(BF) for t in found]
    parts = [jnp.concatenate(split(a), axis=1) for a in systems]
    rest = [
        eye - t.astype(F32) - dot(a, jnp.concatenate([t, t], axis=0)) for a, t in zip(parts, near)
    ]
    return [t.astype(F32) + dot(t, r.astype(BF)) for t, r in zip(near, rest)]


def fixed(shape):
    return pl.BlockSpec(shape, lambda i, s: (0,) * len(shape))


def columns(shape, block):
    return pl.BlockSpec(shape, lambda i, s: (0, block))


def by_step(columns):
    return pl.BlockSpec((STEP, columns), lambda i, s: (i, 0))


def block_columns(block):
    return pl.ds(pl.multiple_of(block * DK, DK), DK)


def fetch_weights(sp, parts, halves, weights, sems):
    z, mine = sp[0], lax.rem(sp[1], 2)
    copies = []
    for side in range(2):
        rows = mine if side == 0 else 1 - mine
        for k in range(NZ):
            part = parts[NZ * side + k]
            place = lax.rem(z - k + NZ, NZ)
            top = pl.multiple_of(rows * ROWS, 128)
            copies.append((part.at[pl.ds(0, ROWS)], weights.at[pl.ds(top, ROWS), block_columns(sp[3 + place])]))
            copies.append((part.at[pl.ds(ROWS, PACK)], halves.at[rows, place]))
    copies = [pltpu.make_async_copy(s, d, sems.at[i]) for i, (s, d) in enumerate(copies)]
    for copy in copies:
        copy.start()
    for copy in copies:
        copy.wait()
    for rows in range(2):
        for b in range(2):
            pair = [halves[rows, sp[9 + 2 * b + side]] for side in range(2)]
            cols = block_columns(sp[7 + b])
            weights[pl.ds(ROWS * rows, PACK), cols] = jnp.concatenate(
                [u[:, :UNIT] for u in pair], axis=1
            )
            weights[pl.ds(ROWS * rows + PACK, PACK), cols] = jnp.concatenate(
                [u[:, UNIT:] for u in pair], axis=1
            )


def params():
    return pltpu.CompilerParams(vmem_limit_bytes=VMEM_LIMIT)


def cost(flops, size):
    return pl.CostEstimate(flops=int(flops), bytes_accessed=int(size), transcendentals=0)


def gate_kernel(
    sp, tokens, wsmall, decay_up, gate_up, rate, scale, log_o, beta_o, gate_o
):
    head = sp[2]
    small = dot(tokens[...], wsmall[...])
    decay_low = small[:, :128].astype(BF)
    gate_low = small[:, 128:256].astype(BF)
    beta_all = scale[...] * sigmoid(small[:, 256:])
    logdec = -rate[...] * sigmoid(dot(decay_low, decay_up[...]))
    gate_o[...] = sigmoid(dot(gate_low, gate_up[...]))
    rows = lax.broadcasted_iota(jnp.int32, (SHARD, SHARD), 0)
    cols = lax.broadcasted_iota(jnp.int32, (SHARD, SHARD), 1)
    ones_low = jnp.where(rows >= cols, 1.0, 0.0).astype(BF)
    ones_twice = jnp.concatenate([ones_low, ones_low], axis=1)
    high, low = split(logdec)
    for blk in range(STEP // SHARD):
        ts = slice(SHARD * blk, SHARD * blk + SHARD)
        log_o[ts] = dot(ones_twice, jnp.concatenate([high[ts], low[ts]], axis=0))
    lane = lax.broadcasted_iota(jnp.int32, (STEP, 128), 1)
    for h in range(2):
        mine = jnp.sum(jnp.where(lane == head + 4 * h, beta_all, 0.0), axis=1, keepdims=True)
        beta_o[:, DK * h : DK * h + DK] = jnp.broadcast_to(mine, (STEP, DK))


def run_gates(sp, tokens, wsmall, decay_up, gate_up, rate, scale):
    wide = jax.ShapeDtypeStruct((GROUP, 2 * DK), F32)
    return pl.pallas_call(
        gate_kernel,
        name="block_gates",
        out_shape=(wide, wide, wide),
        grid_spec=pltpu.PrefetchScalarGridSpec(
            num_scalar_prefetch=1,
            grid=(GROUP // STEP,),
            in_specs=[
                by_step(D),
                fixed((D, 384)),
                fixed((128, 256)),
                fixed((128, 256)),
                fixed((1, 256)),
                fixed((1, 128)),
            ],
            out_specs=[by_step(2 * DK)] * 3,
        ),
        compiler_params=params(),
        cost_estimate=cost(2e9, 1e7),
    )(sp, tokens, wsmall, decay_up, gate_up, rate, scale)


def active(mixed, cols, taps):
    total = taps[0:1] * mixed[5 : 5 + STEP, cols]
    for j in range(1, CONV):
        total = total + taps[j : j + 1] * mixed[5 + j : 5 + j + STEP, cols]
    return total * sigmoid(total)


def state_kernel(sp, tokens, halo, log_sums, betas, conv_k, conv_v, *rest):
    parts = rest[:8]
    down_o, solved_o, carry_o, wq_o, state_o, offset_o = rest[8:14]
    halves, wbuf, mixed, state, sems = rest[14:]
    step = pl.program_id(0)

    @pl.when(step == 0)
    def _():
        fetch_weights(sp, parts, halves, wbuf, sems)
        wq_o[...] = wbuf[:, : 2 * DK]
        before = dot(halo[...], wbuf[:, 2 * DK :]).astype(BF).astype(F32)
        mixed[0:8] = before[8:16]
        rr = lax.broadcasted_iota(jnp.int32, (DK, 2 * DK), 0)
        cc = lax.broadcasted_iota(jnp.int32, (DK, 2 * DK), 1)
        start = jnp.where(rr == cc, 1.0, 0.0)
        state[0] = start
        state[1] = start

    mixed[8:] = dot(tokens[...], wbuf[:, 2 * DK :]).astype(BF).astype(F32)
    keys = active(mixed, slice(0, 256), conv_k)
    values = active(mixed, slice(256, 512), conv_v)
    mixed[0:8] = mixed[STEP : STEP + 8]

    rows = lax.broadcasted_iota(jnp.int32, (SHARD, SHARD), 0)
    cols = lax.broadcasted_iota(jnp.int32, (SHARD, SHARD), 1)
    places = [
        (h, blk, slice(SHARD * blk, SHARD * blk + SHARD), slice(DK * h, DK * h + DK))
        for blk in range(STEP // SHARD)
        for h in range(2)
    ]
    systems, sides, ends, tails = [], [], [], []
    for h, blk, ts, hs in places:
        k, beta, log_sum = keys[ts, hs], betas[ts, hs], log_sums[ts, hs]
        k = k * lax.rsqrt(jnp.sum(k * k, axis=1, keepdims=True) + 1e-06)
        end = log_sum[SHARD - 1 : SHARD]
        k_up = k * jnp.exp(log_sum)
        k_down = k * jnp.exp(-log_sum)
        down_o[ts, hs] = k_down
        systems.append(jnp.where(rows > cols, mm3_nt(k_up, k_down), 0.0) * beta)
        sides.append(jnp.concatenate([k_up * beta, values[ts, hs] * beta], axis=1))
        ends.append((k * jnp.exp(end - log_sum)).T)
        tails.append(jnp.where(rows == cols, jnp.exp(end), 0.0))
    inverses = unit_lower_inverses(systems, rows, cols)
    solved = [mm3(t, r) for t, r in zip(inverses, sides)]
    moves = [mm3(e, s) for e, s in zip(ends, solved)]
    for (h, blk, ts, hs), tail, sol, move in zip(places, tails, solved, moves):
        solved_o[ts, 2 * DK * h : 2 * DK * h + 2 * DK] = sol
        carry = state[h]
        carry_o[ts, 2 * DK * h : 2 * DK * h + 2 * DK] = carry
        new = mm3(tail - move[:, :DK], carry)
        state[h, :, :DK] = new[:, :DK]
        state[h, :, DK:] = new[:, DK:] + move[:, DK:]

    @pl.when(step == pl.num_programs(0) - 1)
    def _():
        state_o[...] = state[...]
        offset_o[...] = state[:, :, DK:]


def run_state(sp, tokens, halo, log_sums, betas, conv, parts):
    return pl.pallas_call(
        state_kernel,
        name="block_state",
        out_shape=(
            jax.ShapeDtypeStruct((GROUP, 2 * DK), F32),
            jax.ShapeDtypeStruct((GROUP, 4 * DK), F32),
            jax.ShapeDtypeStruct((GROUP, 4 * DK), F32),
            jax.ShapeDtypeStruct((D, 2 * DK), BF),
            jax.ShapeDtypeStruct((2, DK, 2 * DK), F32),
            jax.ShapeDtypeStruct((2, DK, DK), F32),
        ),
        grid_spec=pltpu.PrefetchScalarGridSpec(
            num_scalar_prefetch=1,
            grid=(GROUP // STEP,),
            in_specs=[
                by_step(D),
                fixed((16, D)),
                by_step(2 * DK),
                by_step(2 * DK),
                columns((CONV, 256), 1),
                columns((CONV, 256), 2),
            ]
            + [pl.BlockSpec(memory_space=pl.ANY)] * 8,
            out_specs=[
                by_step(2 * DK),
                by_step(4 * DK),
                by_step(4 * DK),
                fixed((D, 2 * DK)),
                fixed((2, DK, 2 * DK)),
                fixed((2, DK, DK)),
            ],
            scratch_shapes=[
                pltpu.VMEM((2, NZ, PACK, 128), BF),
                pltpu.VMEM((D, 6 * DK), BF),
                pltpu.VMEM((8 + STEP, 512), F32),
                pltpu.VMEM((2, DK, 2 * DK), F32),
                pltpu.SemaphoreType.DMA((16,)),
            ],
        ),
        compiler_params=params(),
        cost_estimate=cost(1e10, 2e7),
    )(sp, tokens, halo, log_sums, betas, conv, conv, *parts)


def query_kernel(
    sp, tokens, halo, wq, conv_q, log_sums, k_downs, solved, carries, qeff_o, core_o, mixed
):
    @pl.when(pl.program_id(0) == 0)
    def _():
        before = dot(halo[...], wq[...]).astype(BF).astype(F32)
        mixed[0:8] = before[8:16]

    mixed[8:] = dot(tokens[...], wq[...]).astype(BF).astype(F32)
    query = active(mixed, slice(0, 256), conv_q)
    mixed[0:8] = mixed[STEP : STEP + 8]
    rows = lax.broadcasted_iota(jnp.int32, (SHARD, SHARD), 0)
    cols = lax.broadcasted_iota(jnp.int32, (SHARD, SHARD), 1)
    places = [
        (
            slice(SHARD * blk, SHARD * blk + SHARD),
            slice(DK * h, DK * h + DK),
            slice(2 * DK * h, 2 * DK * h + 2 * DK),
        )
        for blk in range(STEP // SHARD)
        for h in range(2)
    ]
    ups = []
    for ts, hs, _ in places:
        q = query[ts, hs]
        q = q * (lax.rsqrt(jnp.sum(q * q, axis=1, keepdims=True) + 1e-06) * DK**-0.5)
        ups.append(q * jnp.exp(log_sums[ts, hs]))
    scores = [mm3_nt(u, k_downs[ts, hs]) for u, (ts, hs, _) in zip(ups, places)]
    attends = [jnp.where(rows >= cols, a, 0.0) for a in scores]
    withins = [mm3(a, solved[ts, both]) for a, (ts, _, both) in zip(attends, places)]
    outs = [
        mm3(u - w[:, :DK], carries[ts, both]) for u, w, (ts, _, both) in zip(ups, withins, places)
    ]
    for out, w, (ts, hs, _) in zip(outs, withins, places):
        qeff_o[ts, hs] = out[:, :DK]
        core_o[ts, hs] = out[:, DK:] + w[:, DK:]


def run_queries(sp, tokens, halo, wq, conv, log_sums, k_downs, solved, carries):
    wide = jax.ShapeDtypeStruct((GROUP, 2 * DK), F32)
    return pl.pallas_call(
        query_kernel,
        name="block_query",
        out_shape=(wide, wide),
        grid_spec=pltpu.PrefetchScalarGridSpec(
            num_scalar_prefetch=1,
            grid=(GROUP // STEP,),
            in_specs=[
                by_step(D),
                fixed((16, D)),
                fixed((D, 2 * DK)),
                columns((CONV, 256), 0),
                by_step(2 * DK),
                by_step(2 * DK),
                by_step(4 * DK),
                by_step(4 * DK),
            ],
            out_specs=[by_step(2 * DK)] * 2,
            scratch_shapes=[pltpu.VMEM((8 + STEP, 256), F32)],
        ),
        compiler_params=params(),
        cost_estimate=cost(5e9, 2e7),
    )(sp, tokens, halo, wq, conv, log_sums, k_downs, solved, carries)


def finish_kernel(near, middle, far, qeff, core, gate, gain, out, state):
    heads = range(2)

    @pl.when(pl.program_id(0) == 0)
    def _():
        carries = [middle[h, :, DK:] + mm3(middle[h, :, :DK], far[h]) for h in heads]
        starts = [near[h, :, DK:] + mm3(near[h, :, :DK], carries[h]) for h in heads]
        for h in heads:
            state[h] = starts[h]

    spans = [slice(DK * h, DK * h + DK) for h in heads]
    added = [mm3(qeff[:, hs], state[h]) for h, hs in zip(heads, spans)]
    for hs, more in zip(spans, added):
        full = core[:, hs] + more
        scale = lax.rsqrt(jnp.mean(full * full, axis=1, keepdims=True) + 1e-06)
        out[:, hs] = (full * scale * gain[...] * gate[:, hs]).astype(BF)


def run_finish(near, middle, far, qeff, core, gate, gain):
    def whole(shape):
        return pl.BlockSpec(shape, lambda i: (0,) * len(shape))

    tile = pl.BlockSpec((512, 2 * DK), lambda i: (i, 0))
    return pl.pallas_call(
        finish_kernel,
        name="finish",
        out_shape=jax.ShapeDtypeStruct((GROUP, 2 * DK), BF),
        grid=(GROUP // 512,),
        in_specs=[
            whole((2, DK, 2 * DK)),
            whole((2, DK, 2 * DK)),
            whole((2, DK, DK)),
            tile,
            tile,
            tile,
            whole((1, DK)),
        ],
        out_specs=tile,
        scratch_shapes=[pltpu.VMEM((2, DK, DK), F32)],
        compiler_params=pltpu.CompilerParams(vmem_limit_bytes=VMEM_LIMIT),
    )(near, middle, far, qeff, core, gate, gain)


def gather_weights(weight, c, y):
    rows = lax.dynamic_slice(weight, (ROWS * lax.rem(y, 2), 0), (ROWS, 3 * UNIT))
    whole = jnp.where(c == 0, rows[:, : 2 * UNIT], rows[:, UNIT:])
    half = jnp.where(c == 0, rows[:, 2 * UNIT :], rows[:, :UNIT])
    half = jnp.concatenate([half[:PACK], half[PACK:]], axis=1)
    seq = ("z", "x", "c")
    mine = jnp.concatenate(
        [lax.ppermute(whole, seq, WHOLE_ROUTE), lax.ppermute(half, seq, HALF_ROUTE)], axis=0
    )
    near = [mine] + [lax.ppermute(mine, "z", ring(k)) for k in range(1, NZ)]
    return near, [lax.ppermute(p, "y", ring(d)) for p, d in zip(near, (1, 3, 1, 3))]


def per_device(
    tokens,
    qkv_weight,
    conv_weight,
    decay_down,
    decay_up,
    decay_rate,
    beta_weight,
    beta_scale,
    gate_down,
    gate_up,
    norm_gain,
):
    z, x, c, y = (lax.axis_index(a) for a in ("z", "x", "c", "y"))
    g = x * NC + c
    wsmall = jnp.concatenate(
        [decay_down, gate_down, jnp.pad(beta_weight, ((0, 0), (0, 128 - H)))], axis=1
    )
    head = first_head(x, c)
    sp = jnp.concatenate([jnp.stack([z, y, head]).astype(jnp.int32), jnp.asarray(TABLES)[g]])

    def mine(array, start=0):
        return jnp.concatenate(
            [
                lax.dynamic_slice(array, (0, start + DK * (head + 4 * h)), (array.shape[0], DK))
                for h in range(2)
            ],
            axis=1,
        )

    taps = jnp.concatenate([mine(conv_weight, HV * kind) for kind in range(3)], axis=1)
    scale = jnp.pad(beta_scale, (0, 128 - H)).reshape(1, 128)
    row = lax.all_gather(tokens, ("x", "c"), axis=0, tiled=True)
    near, far = gather_weights(qkv_weight, c, y)
    halo = lax.ppermute(row[GROUP - 16 :], "z", ahead(1))
    log_sums, betas, gate = run_gates(
        sp,
        row,
        wsmall,
        mine(decay_up),
        mine(gate_up),
        mine(decay_rate.reshape(1, HV)),
        scale,
    )
    k_downs, solved, carries, wq, state, offset = run_state(
        sp, row, halo, log_sums, betas, taps, near + far
    )
    first = lax.ppermute(state, "z", ahead(1))
    second = lax.ppermute(state, "z", ahead(2))
    third = lax.ppermute(offset, "z", ahead(3))
    qeff, core = run_queries(sp, row, halo, wq, taps, log_sums, k_downs, solved, carries)
    out = run_finish(first, second, third, qeff, core, gate, norm_gain.reshape(1, DK))
    out = lax.all_to_all(out.reshape(ROW, SHARD, 2 * DK), ("x", "c"), 0, 0)
    heads = {
        first_head(i // NC, i % NC) + 4 * h: out[i, :, DK * h : DK * h + DK]
        for i in range(ROW)
        for h in range(2)
    }
    return jnp.concatenate([heads[h] for h in range(H)], axis=1)


def solution(mesh):
    fine = Mesh(mesh.devices.reshape(NZ, NX, NC, NY), ("z", "x", "c", "y"))
    seq = ("z", "x", "c")
    in_specs = (P(("y",) + seq, None), P(None, seq)) + (P(),) * 9
    return jax.shard_map(
        per_device,
        mesh=fine,
        in_specs=in_specs,
        out_specs=P(("y",) + seq, None),
        check_vma=False,
    )
```

```python
import itertools

import jax
import jax.numpy as jnp
import numpy as np
from jax import lax
from jax.experimental import pallas as pl
from jax.experimental.pallas import tpu as pltpu
from jax.sharding import Mesh
from jax.sharding import PartitionSpec as P

H = 16
DK = 128
CONV = 4
D = 2304
HV = H * DK
BF = jnp.bfloat16
F32 = jnp.float32

NZ, NX, NC, NY = 4, 4, 2, 4
ROW = NX * NC
SHARD = 128
GROUP = ROW * SHARD
UNIT = 64
ROWS = D // 2
PACK = ROWS // 2
GATE_STEP = 4 * SHARD
STATE_STEP = 8 * SHARD
QUERY_STEP = 2 * SHARD
VMEM_LIMIT = 56 * 1024 * 1024


def nearest(sources):
    def way(order):
        return sum(min((order[i] - sources[i] // ROW) % 4, (sources[i] // ROW - order[i]) % 4) for i in range(4))

    return min(itertools.permutations(range(4)), key=way)


def first_head(x, c):
    return (x ^ 1) + 8 * c


def block_plan():
    whole_route, half_route, tables = [], [], []
    for group in range(ROW):
        head = first_head(group // NC, group % NC)
        blocks = [(kind, hp, 16 * kind + head + 4 * hp) for kind in range(3) for hp in range(2)]
        whole = [b for b in blocks if b[2] % 3 != 1]
        halves = [b for b in blocks if b[2] % 3 == 1]
        sources = [2 * (m // 3) + (m % 3) // 2 for _, _, m in whole]
        order = nearest(sources)
        at_z = [0] * 4
        for place, source, (kind, hp, _) in zip(order, sources, whole):
            whole_route.append((source, place * ROW + group))
            at_z[place] = 2 * kind + hp
        sources = [2 * (m // 3) + side for _, _, m in halves for side in range(2)]
        order = nearest(sources)
        for place, source in zip(order, sources):
            half_route.append((source, place * ROW + group))
        tables.append(at_z + [2 * kind + hp for kind, hp, _ in halves] + list(order))
    return sorted(whole_route), sorted(half_route), np.asarray(tables, np.int32)


WHOLE_ROUTE, HALF_ROUTE, TABLES = block_plan()


def ring(distance, size=4):
    return [(i, (i + distance) % size) for i in range(size)]


def ahead(distance, size=4):
    return [(i, i + distance) for i in range(size - distance)]


def split(x):
    high = x.astype(BF)
    return high, (x - high.astype(F32)).astype(BF)


def dot(a, b):
    return lax.dot_general(a, b, (((1,), (0,)), ((), ())), preferred_element_type=F32)


def dot_nt(a, b):
    return lax.dot_general(a, b, (((1,), (1,)), ((), ())), preferred_element_type=F32)


def mm3(a, b):
    ah, al = split(a)
    bh, bl = split(b)
    return dot(jnp.concatenate([ah, al, ah], axis=1), jnp.concatenate([bh, bh, bl], axis=0))


def mm3_nt(a, b):
    ah, al = split(a)
    bh, bl = split(b)
    return dot_nt(jnp.concatenate([ah, al, ah], axis=1), jnp.concatenate([bh, bh, bl], axis=1))


def sigmoid(x):
    return 1.0 / (1.0 + jnp.exp(-x))


def unit_lower_inverses(systems, rows, cols):
    eye = jnp.where(rows == cols, 1.0, 0.0)
    pair = (rows // 2) == (cols // 2)
    found = [eye - jnp.where(pair, a, 0.0) for a in systems]
    size = 2
    while size < SHARD:
        band = ((rows // (2 * size)) == (cols // (2 * size))) & ((rows // size) != (cols // size))
        low = [jnp.where(band, a, 0.0).astype(BF) for a in systems]
        near = [t.astype(BF) for t in found]
        half = [dot(t, a).astype(BF) for t, a in zip(near, low)]
        step = [dot(p, t) for p, t in zip(half, near)]
        found = [t - s for t, s in zip(found, step)]
        size *= 2
    near = [t.astype(BF) for t in found]
    parts = [jnp.concatenate(split(a), axis=1) for a in systems]
    rest = [
        eye - t.astype(F32) - dot(a, jnp.concatenate([t, t], axis=0)) for a, t in zip(parts, near)
    ]
    return [t.astype(F32) + dot(t, r.astype(BF)) for t, r in zip(near, rest)]


def fixed(shape):
    return pl.BlockSpec(shape, lambda i, s: (0,) * len(shape))


def columns(shape, block):
    return pl.BlockSpec(shape, lambda i, s: (0, block))


def by_step(step, columns):
    return pl.BlockSpec((step, columns), lambda i, s: (i, 0))


def block_columns(block):
    return pl.ds(pl.multiple_of(block * DK, DK), DK)


def fetch_weights(sp, parts, halves, weights, sems):
    z, mine = sp[0], lax.rem(sp[1], 2)
    copies = []
    for side in range(2):
        rows = mine if side == 0 else 1 - mine
        for k in range(NZ):
            part = parts[NZ * side + k]
            place = lax.rem(z - k + NZ, NZ)
            top = pl.multiple_of(rows * ROWS, 128)
            copies.append((part.at[pl.ds(0, ROWS)], weights.at[pl.ds(top, ROWS), block_columns(sp[3 + place])]))
            copies.append((part.at[pl.ds(ROWS, PACK)], halves.at[rows, place]))
    copies = [pltpu.make_async_copy(s, d, sems.at[i]) for i, (s, d) in enumerate(copies)]
    for copy in copies:
        copy.start()
    for copy in copies:
        copy.wait()
    for rows in range(2):
        for b in range(2):
            pair = [halves[rows, sp[9 + 2 * b + side]] for side in range(2)]
            cols = block_columns(sp[7 + b])
            weights[pl.ds(ROWS * rows, PACK), cols] = jnp.concatenate(
                [u[:, :UNIT] for u in pair], axis=1
            )
            weights[pl.ds(ROWS * rows + PACK, PACK), cols] = jnp.concatenate(
                [u[:, UNIT:] for u in pair], axis=1
            )


def params():
    return pltpu.CompilerParams(vmem_limit_bytes=VMEM_LIMIT)


def cost(flops, size):
    return pl.CostEstimate(flops=int(flops), bytes_accessed=int(size), transcendentals=0)


def gate_kernel(
    sp, tokens, wsmall, decay_up, gate_up, rate, scale, log_o, beta_o, gate_o
):
    head = sp[2]
    small = dot(tokens[...], wsmall[...])
    decay_low = small[:, :128].astype(BF)
    gate_low = small[:, 128:256].astype(BF)
    beta_all = scale[...] * sigmoid(small[:, 256:])
    logdec = -rate[...] * sigmoid(dot(decay_low, decay_up[...]))
    gate_o[...] = sigmoid(dot(gate_low, gate_up[...]))
    rows = lax.broadcasted_iota(jnp.int32, (SHARD, SHARD), 0)
    cols = lax.broadcasted_iota(jnp.int32, (SHARD, SHARD), 1)
    ones_low = jnp.where(rows >= cols, 1.0, 0.0).astype(BF)
    ones_twice = jnp.concatenate([ones_low, ones_low], axis=1)
    high, low = split(logdec)
    for blk in range(GATE_STEP // SHARD):
        ts = slice(SHARD * blk, SHARD * blk + SHARD)
        log_o[ts] = dot(ones_twice, jnp.concatenate([high[ts], low[ts]], axis=0))
    lane = lax.broadcasted_iota(jnp.int32, (GATE_STEP, 128), 1)
    for h in range(2):
        mine = jnp.sum(jnp.where(lane == head + 4 * h, beta_all, 0.0), axis=1, keepdims=True)
        beta_o[:, DK * h : DK * h + DK] = jnp.broadcast_to(mine, (GATE_STEP, DK))


def run_gates(sp, tokens, wsmall, decay_up, gate_up, rate, scale):
    wide = jax.ShapeDtypeStruct((GROUP, 2 * DK), F32)
    return pl.pallas_call(
        gate_kernel,
        name="block_gates",
        out_shape=(wide, wide, wide),
        grid_spec=pltpu.PrefetchScalarGridSpec(
            num_scalar_prefetch=1,
            grid=(GROUP // GATE_STEP,),
            in_specs=[
                by_step(GATE_STEP, D),
                fixed((D, 384)),
                fixed((128, 256)),
                fixed((128, 256)),
                fixed((1, 256)),
                fixed((1, 128)),
            ],
            out_specs=[by_step(GATE_STEP, 2 * DK)] * 3,
        ),
        compiler_params=params(),
        cost_estimate=cost(2e9, 1e7),
    )(sp, tokens, wsmall, decay_up, gate_up, rate, scale)


def active(mixed, cols, taps):
    count = mixed.shape[0] - 8
    total = taps[0:1] * mixed[5 : 5 + count, cols]
    for j in range(1, CONV):
        total = total + taps[j : j + 1] * mixed[5 + j : 5 + j + count, cols]
    return total * sigmoid(total)


def state_kernel(sp, tokens, halo, log_sums, betas, conv_k, conv_v, *rest):
    parts = rest[:8]
    down_o, solved_o, carry_o, wq_o, state_o, offset_o = rest[8:14]
    halves, wbuf, mixed, state, sems = rest[14:]
    step = pl.program_id(0)

    @pl.when(step == 0)
    def _():
        fetch_weights(sp, parts, halves, wbuf, sems)
        wq_o[...] = wbuf[:, : 2 * DK]
        before = dot(halo[...], wbuf[:, 2 * DK :]).astype(BF).astype(F32)
        mixed[0:8] = before[8:16]
        rr = lax.broadcasted_iota(jnp.int32, (DK, 2 * DK), 0)
        cc = lax.broadcasted_iota(jnp.int32, (DK, 2 * DK), 1)
        start = jnp.where(rr == cc, 1.0, 0.0)
        state[0] = start
        state[1] = start

    mixed[8:] = dot(tokens[...], wbuf[:, 2 * DK :]).astype(BF).astype(F32)
    keys = active(mixed, slice(0, 256), conv_k)
    values = active(mixed, slice(256, 512), conv_v)
    mixed[0:8] = mixed[STATE_STEP : STATE_STEP + 8]

    rows = lax.broadcasted_iota(jnp.int32, (SHARD, SHARD), 0)
    cols = lax.broadcasted_iota(jnp.int32, (SHARD, SHARD), 1)
    places = [
        (h, blk, slice(SHARD * blk, SHARD * blk + SHARD), slice(DK * h, DK * h + DK))
        for blk in range(STATE_STEP // SHARD)
        for h in range(2)
    ]
    systems, sides, ends, tails = [], [], [], []
    for h, blk, ts, hs in places:
        k, beta, log_sum = keys[ts, hs], betas[ts, hs], log_sums[ts, hs]
        k = k * lax.rsqrt(jnp.sum(k * k, axis=1, keepdims=True) + 1e-06)
        end = log_sum[SHARD - 1 : SHARD]
        k_up = k * jnp.exp(log_sum)
        k_down = k * jnp.exp(-log_sum)
        down_o[ts, hs] = k_down
        systems.append(jnp.where(rows > cols, mm3_nt(k_up, k_down), 0.0) * beta)
        sides.append(jnp.concatenate([k_up * beta, values[ts, hs] * beta], axis=1))
        ends.append((k * jnp.exp(end - log_sum)).T)
        tails.append(jnp.where(rows == cols, jnp.exp(end), 0.0))
    inverses = unit_lower_inverses(systems, rows, cols)
    solved = [mm3(t, r) for t, r in zip(inverses, sides)]
    moves = [mm3(e, s) for e, s in zip(ends, solved)]
    for (h, blk, ts, hs), tail, sol, move in zip(places, tails, solved, moves):
        solved_o[ts, 2 * DK * h : 2 * DK * h + 2 * DK] = sol
        carry = state[h]
        carry_o[ts, 2 * DK * h : 2 * DK * h + 2 * DK] = carry
        new = mm3(tail - move[:, :DK], carry)
        state[h, :, :DK] = new[:, :DK]
        state[h, :, DK:] = new[:, DK:] + move[:, DK:]

    @pl.when(step == pl.num_programs(0) - 1)
    def _():
        state_o[...] = state[...]
        offset_o[...] = state[:, :, DK:]


def run_state(sp, tokens, halo, log_sums, betas, conv, parts):
    return pl.pallas_call(
        state_kernel,
        name="block_state",
        out_shape=(
            jax.ShapeDtypeStruct((GROUP, 2 * DK), F32),
            jax.ShapeDtypeStruct((GROUP, 4 * DK), F32),
            jax.ShapeDtypeStruct((GROUP, 4 * DK), F32),
            jax.ShapeDtypeStruct((D, 2 * DK), BF),
            jax.ShapeDtypeStruct((2, DK, 2 * DK), F32),
            jax.ShapeDtypeStruct((2, DK, DK), F32),
        ),
        grid_spec=pltpu.PrefetchScalarGridSpec(
            num_scalar_prefetch=1,
            grid=(GROUP // STATE_STEP,),
            in_specs=[
                by_step(STATE_STEP, D),
                fixed((16, D)),
                by_step(STATE_STEP, 2 * DK),
                by_step(STATE_STEP, 2 * DK),
                columns((CONV, 256), 1),
                columns((CONV, 256), 2),
            ]
            + [pl.BlockSpec(memory_space=pl.ANY)] * 8,
            out_specs=[
                by_step(STATE_STEP, 2 * DK),
                by_step(STATE_STEP, 4 * DK),
                by_step(STATE_STEP, 4 * DK),
                fixed((D, 2 * DK)),
                fixed((2, DK, 2 * DK)),
                fixed((2, DK, DK)),
            ],
            scratch_shapes=[
                pltpu.VMEM((2, NZ, PACK, 128), BF),
                pltpu.VMEM((D, 6 * DK), BF),
                pltpu.VMEM((8 + STATE_STEP, 512), F32),
                pltpu.VMEM((2, DK, 2 * DK), F32),
                pltpu.SemaphoreType.DMA((16,)),
            ],
        ),
        compiler_params=params(),
        cost_estimate=cost(1e10, 2e7),
    )(sp, tokens, halo, log_sums, betas, conv, conv, *parts)


def query_kernel(
    sp, tokens, halo, wq, conv_q, log_sums, k_downs, solved, carries, qeff_o, core_o, mixed
):
    @pl.when(pl.program_id(0) == 0)
    def _():
        before = dot(halo[...], wq[...]).astype(BF).astype(F32)
        mixed[0:8] = before[8:16]

    mixed[8:] = dot(tokens[...], wq[...]).astype(BF).astype(F32)
    query = active(mixed, slice(0, 256), conv_q)
    mixed[0:8] = mixed[QUERY_STEP : QUERY_STEP + 8]
    rows = lax.broadcasted_iota(jnp.int32, (SHARD, SHARD), 0)
    cols = lax.broadcasted_iota(jnp.int32, (SHARD, SHARD), 1)
    places = [
        (
            slice(SHARD * blk, SHARD * blk + SHARD),
            slice(DK * h, DK * h + DK),
            slice(2 * DK * h, 2 * DK * h + 2 * DK),
        )
        for blk in range(QUERY_STEP // SHARD)
        for h in range(2)
    ]
    ups = []
    for ts, hs, _ in places:
        q = query[ts, hs]
        q = q * (lax.rsqrt(jnp.sum(q * q, axis=1, keepdims=True) + 1e-06) * DK**-0.5)
        ups.append(q * jnp.exp(log_sums[ts, hs]))
    scores = [mm3_nt(u, k_downs[ts, hs]) for u, (ts, hs, _) in zip(ups, places)]
    attends = [jnp.where(rows >= cols, a, 0.0) for a in scores]
    withins = [mm3(a, solved[ts, both]) for a, (ts, _, both) in zip(attends, places)]
    outs = [
        mm3(u - w[:, :DK], carries[ts, both]) for u, w, (ts, _, both) in zip(ups, withins, places)
    ]
    for out, w, (ts, hs, _) in zip(outs, withins, places):
        qeff_o[ts, hs] = out[:, :DK]
        core_o[ts, hs] = out[:, DK:] + w[:, DK:]


def run_queries(sp, tokens, halo, wq, conv, log_sums, k_downs, solved, carries):
    wide = jax.ShapeDtypeStruct((GROUP, 2 * DK), F32)
    return pl.pallas_call(
        query_kernel,
        name="block_query",
        out_shape=(wide, wide),
        grid_spec=pltpu.PrefetchScalarGridSpec(
            num_scalar_prefetch=1,
            grid=(GROUP // QUERY_STEP,),
            in_specs=[
                by_step(QUERY_STEP, D),
                fixed((16, D)),
                fixed((D, 2 * DK)),
                columns((CONV, 256), 0),
                by_step(QUERY_STEP, 2 * DK),
                by_step(QUERY_STEP, 2 * DK),
                by_step(QUERY_STEP, 4 * DK),
                by_step(QUERY_STEP, 4 * DK),
            ],
            out_specs=[by_step(QUERY_STEP, 2 * DK)] * 2,
            scratch_shapes=[pltpu.VMEM((8 + QUERY_STEP, 256), F32)],
        ),
        compiler_params=params(),
        cost_estimate=cost(5e9, 2e7),
    )(sp, tokens, halo, wq, conv, log_sums, k_downs, solved, carries)


def finish_kernel(near, middle, far, qeff, core, gate, gain, out, state):
    heads = range(2)

    @pl.when(pl.program_id(0) == 0)
    def _():
        carries = [middle[h, :, DK:] + mm3(middle[h, :, :DK], far[h]) for h in heads]
        starts = [near[h, :, DK:] + mm3(near[h, :, :DK], carries[h]) for h in heads]
        for h in heads:
            state[h] = starts[h]

    spans = [slice(DK * h, DK * h + DK) for h in heads]
    added = [mm3(qeff[:, hs], state[h]) for h, hs in zip(heads, spans)]
    for hs, more in zip(spans, added):
        full = core[:, hs] + more
        scale = lax.rsqrt(jnp.mean(full * full, axis=1, keepdims=True) + 1e-06)
        out[:, hs] = (full * scale * gain[...] * gate[:, hs]).astype(BF)


def run_finish(near, middle, far, qeff, core, gate, gain):
    def whole(shape):
        return pl.BlockSpec(shape, lambda i: (0,) * len(shape))

    tile = pl.BlockSpec((512, 2 * DK), lambda i: (i, 0))
    return pl.pallas_call(
        finish_kernel,
        name="finish",
        out_shape=jax.ShapeDtypeStruct((GROUP, 2 * DK), BF),
        grid=(GROUP // 512,),
        in_specs=[
            whole((2, DK, 2 * DK)),
            whole((2, DK, 2 * DK)),
            whole((2, DK, DK)),
            tile,
            tile,
            tile,
            whole((1, DK)),
        ],
        out_specs=tile,
        scratch_shapes=[pltpu.VMEM((2, DK, DK), F32)],
        compiler_params=pltpu.CompilerParams(vmem_limit_bytes=VMEM_LIMIT),
    )(near, middle, far, qeff, core, gate, gain)


def gather_weights(weight, c, y):
    rows = lax.dynamic_slice(weight, (ROWS * lax.rem(y, 2), 0), (ROWS, 3 * UNIT))
    whole = jnp.where(c == 0, rows[:, : 2 * UNIT], rows[:, UNIT:])
    half = jnp.where(c == 0, rows[:, 2 * UNIT :], rows[:, :UNIT])
    half = jnp.concatenate([half[:PACK], half[PACK:]], axis=1)
    seq = ("z", "x", "c")
    mine = jnp.concatenate(
        [lax.ppermute(whole, seq, WHOLE_ROUTE), lax.ppermute(half, seq, HALF_ROUTE)], axis=0
    )
    near = [mine] + [lax.ppermute(mine, "z", ring(k)) for k in range(1, NZ)]
    return near, [lax.ppermute(p, "y", ring(d)) for p, d in zip(near, (1, 3, 1, 3))]


def per_device(
    tokens,
    qkv_weight,
    conv_weight,
    decay_down,
    decay_up,
    decay_rate,
    beta_weight,
    beta_scale,
    gate_down,
    gate_up,
    norm_gain,
):
    z, x, c, y = (lax.axis_index(a) for a in ("z", "x", "c", "y"))
    g = x * NC + c
    wsmall = jnp.concatenate(
        [decay_down, gate_down, jnp.pad(beta_weight, ((0, 0), (0, 128 - H)))], axis=1
    )
    head = first_head(x, c)
    sp = jnp.concatenate([jnp.stack([z, y, head]).astype(jnp.int32), jnp.asarray(TABLES)[g]])

    def mine(array, start=0):
        return jnp.concatenate(
            [
                lax.dynamic_slice(array, (0, start + DK * (head + 4 * h)), (array.shape[0], DK))
                for h in range(2)
            ],
            axis=1,
        )

    taps = jnp.concatenate([mine(conv_weight, HV * kind) for kind in range(3)], axis=1)
    scale = jnp.pad(beta_scale, (0, 128 - H)).reshape(1, 128)
    row = lax.all_gather(tokens, ("x", "c"), axis=0, tiled=True)
    near, far = gather_weights(qkv_weight, c, y)
    halo = lax.ppermute(row[GROUP - 16 :], "z", ahead(1))
    log_sums, betas, gate = run_gates(
        sp,
        row,
        wsmall,
        mine(decay_up),
        mine(gate_up),
        mine(decay_rate.reshape(1, HV)),
        scale,
    )
    k_downs, solved, carries, wq, state, offset = run_state(
        sp, row, halo, log_sums, betas, taps, near + far
    )
    first = lax.ppermute(state, "z", ahead(1))
    second = lax.ppermute(state, "z", ahead(2))
    third = lax.ppermute(offset, "z", ahead(3))
    qeff, core = run_queries(sp, row, halo, wq, taps, log_sums, k_downs, solved, carries)
    out = run_finish(first, second, third, qeff, core, gate, norm_gain.reshape(1, DK))
    out = lax.all_to_all(out.reshape(ROW, SHARD, 2 * DK), ("x", "c"), 0, 0)
    heads = {
        first_head(i // NC, i % NC) + 4 * h: out[i, :, DK * h : DK * h + DK]
        for i in range(ROW)
        for h in range(2)
    }
    return jnp.concatenate([heads[h] for h in range(H)], axis=1)


def solution(mesh):
    fine = Mesh(mesh.devices.reshape(NZ, NX, NC, NY), ("z", "x", "c", "y"))
    seq = ("z", "x", "c")
    in_specs = (P(("y",) + seq, None), P(None, seq)) + (P(),) * 9
    return jax.shard_map(
        per_device,
        mesh=fine,
        in_specs=in_specs,
        out_specs=P(("y",) + seq, None),
        check_vma=False,
    )
```

```python
import itertools

import jax
import jax.numpy as jnp
import numpy as np
from jax import lax
from jax.experimental import pallas as pl
from jax.experimental.pallas import tpu as pltpu
from jax.sharding import Mesh
from jax.sharding import PartitionSpec as P

H = 16
DK = 128
CONV = 4
D = 2304
HV = H * DK
BF = jnp.bfloat16
F32 = jnp.float32

NZ, NX, NC, NY = 4, 4, 2, 4
ROW = NX * NC
SHARD = 128
GROUP = ROW * SHARD
UNIT = 64
ROWS = D // 2
PACK = ROWS // 2
GATE_STEP = 4 * SHARD
STATE_STEP = 8 * SHARD
QUERY_STEP = 2 * SHARD
VMEM_LIMIT = 56 * 1024 * 1024


def nearest(sources):
    def way(order):
        return sum(min((order[i] - sources[i] // ROW) % 4, (sources[i] // ROW - order[i]) % 4) for i in range(4))

    return min(itertools.permutations(range(4)), key=way)


def first_head(x, c):
    return (x ^ 1) + 8 * c


def block_plan():
    whole_route, half_route, tables = [], [], []
    for group in range(ROW):
        head = first_head(group // NC, group % NC)
        blocks = [(kind, hp, 16 * kind + head + 4 * hp) for kind in range(3) for hp in range(2)]
        whole = [b for b in blocks if b[2] % 3 != 1]
        halves = [b for b in blocks if b[2] % 3 == 1]
        sources = [2 * (m // 3) + (m % 3) // 2 for _, _, m in whole]
        order = nearest(sources)
        at_z = [0] * 4
        for place, source, (kind, hp, _) in zip(order, sources, whole):
            whole_route.append((source, place * ROW + group))
            at_z[place] = 2 * kind + hp
        sources = [2 * (m // 3) + side for _, _, m in halves for side in range(2)]
        order = nearest(sources)
        for place, source in zip(order, sources):
            half_route.append((source, place * ROW + group))
        tables.append(at_z + [2 * kind + hp for kind, hp, _ in halves] + list(order))
    return sorted(whole_route), sorted(half_route), np.asarray(tables, np.int32)


WHOLE_ROUTE, HALF_ROUTE, TABLES = block_plan()


def ring(distance, size=4):
    return [(i, (i + distance) % size) for i in range(size)]


def ahead(distance, size=4):
    return [(i, i + distance) for i in range(size - distance)]


def split(x):
    high = x.astype(BF)
    return high, (x - high.astype(F32)).astype(BF)


def dot(a, b):
    return lax.dot_general(a, b, (((1,), (0,)), ((), ())), preferred_element_type=F32)


def dot_nt(a, b):
    return lax.dot_general(a, b, (((1,), (1,)), ((), ())), preferred_element_type=F32)


def mm3(a, b):
    ah, al = split(a)
    bh, bl = split(b)
    return dot(jnp.concatenate([ah, al, ah], axis=1), jnp.concatenate([bh, bh, bl], axis=0))


def mm3_nt(a, b):
    ah, al = split(a)
    bh, bl = split(b)
    return dot_nt(jnp.concatenate([ah, al, ah], axis=1), jnp.concatenate([bh, bh, bl], axis=1))


def sigmoid(x):
    return 1.0 / (1.0 + jnp.exp(-x))


def unit_lower_inverses(systems, rows, cols):
    eye = jnp.where(rows == cols, 1.0, 0.0)
    pair = (rows // 2) == (cols // 2)
    found = [eye - jnp.where(pair, a, 0.0) for a in systems]
    size = 2
    while size < SHARD:
        band = ((rows // (2 * size)) == (cols // (2 * size))) & ((rows // size) != (cols // size))
        low = [jnp.where(band, a, 0.0).astype(BF) for a in systems]
        near = [t.astype(BF) for t in found]
        half = [dot(t, a).astype(BF) for t, a in zip(near, low)]
        step = [dot(p, t) for p, t in zip(half, near)]
        found = [t - s for t, s in zip(found, step)]
        size *= 2
    near = [t.astype(BF) for t in found]
    parts = [jnp.concatenate(split(a), axis=1) for a in systems]
    rest = [
        eye - t.astype(F32) - dot(a, jnp.concatenate([t, t], axis=0)) for a, t in zip(parts, near)
    ]
    return [t.astype(F32) + dot(t, r.astype(BF)) for t, r in zip(near, rest)]


def fixed(shape):
    return pl.BlockSpec(shape, lambda i, s: (0,) * len(shape))


def columns(shape, block):
    return pl.BlockSpec(shape, lambda i, s: (0, block))


def by_step(step, columns):
    return pl.BlockSpec((step, columns), lambda i, s: (i, 0))


def block_columns(block):
    return pl.ds(pl.multiple_of(block * DK, DK), DK)


def fetch_weights(sp, parts, halves, weights, sems):
    z, mine = sp[0], lax.rem(sp[1], 2)
    copies = []
    for side in range(2):
        rows = mine if side == 0 else 1 - mine
        for k in range(NZ):
            part = parts[NZ * side + k]
            place = lax.rem(z - k + NZ, NZ)
            top = pl.multiple_of(rows * ROWS, 128)
            copies.append((part.at[pl.ds(0, ROWS)], weights.at[pl.ds(top, ROWS), block_columns(sp[3 + place])]))
            split_off = side == 1 and k == 1
            half = parts[2 * NZ] if split_off else part.at[pl.ds(ROWS, PACK)]
            copies.append((half, halves.at[rows, place]))
    copies = [pltpu.make_async_copy(s, d, sems.at[i]) for i, (s, d) in enumerate(copies)]
    for copy in copies:
        copy.start()
    for copy in copies:
        copy.wait()
    for rows in range(2):
        for b in range(2):
            pair = [halves[rows, sp[9 + 2 * b + side]] for side in range(2)]
            cols = block_columns(sp[7 + b])
            weights[pl.ds(ROWS * rows, PACK), cols] = jnp.concatenate(
                [u[:, :UNIT] for u in pair], axis=1
            )
            weights[pl.ds(ROWS * rows + PACK, PACK), cols] = jnp.concatenate(
                [u[:, UNIT:] for u in pair], axis=1
            )


def params():
    return pltpu.CompilerParams(vmem_limit_bytes=VMEM_LIMIT)


def cost(flops, size):
    return pl.CostEstimate(flops=int(flops), bytes_accessed=int(size), transcendentals=0)


def gate_kernel(
    sp, tokens, wsmall, decay_up, gate_up, rate, scale, log_o, beta_o, gate_o
):
    head = sp[2]
    small = dot(tokens[...], wsmall[...])
    decay_low = small[:, :128].astype(BF)
    gate_low = small[:, 128:256].astype(BF)
    beta_all = scale[...] * sigmoid(small[:, 256:])
    logdec = -rate[...] * sigmoid(dot(decay_low, decay_up[...]))
    gate_o[...] = sigmoid(dot(gate_low, gate_up[...]))
    rows = lax.broadcasted_iota(jnp.int32, (SHARD, SHARD), 0)
    cols = lax.broadcasted_iota(jnp.int32, (SHARD, SHARD), 1)
    ones_low = jnp.where(rows >= cols, 1.0, 0.0).astype(BF)
    ones_twice = jnp.concatenate([ones_low, ones_low], axis=1)
    high, low = split(logdec)
    for blk in range(GATE_STEP // SHARD):
        ts = slice(SHARD * blk, SHARD * blk + SHARD)
        log_o[ts] = dot(ones_twice, jnp.concatenate([high[ts], low[ts]], axis=0))
    lane = lax.broadcasted_iota(jnp.int32, (GATE_STEP, 128), 1)
    for h in range(2):
        mine = jnp.sum(jnp.where(lane == head + 4 * h, beta_all, 0.0), axis=1, keepdims=True)
        beta_o[:, DK * h : DK * h + DK] = jnp.broadcast_to(mine, (GATE_STEP, DK))


def run_gates(sp, tokens, wsmall, decay_up, gate_up, rate, scale):
    wide = jax.ShapeDtypeStruct((GROUP, 2 * DK), F32)
    return pl.pallas_call(
        gate_kernel,
        name="block_gates",
        out_shape=(wide, wide, wide),
        grid_spec=pltpu.PrefetchScalarGridSpec(
            num_scalar_prefetch=1,
            grid=(GROUP // GATE_STEP,),
            in_specs=[
                by_step(GATE_STEP, D),
                fixed((D, 384)),
                fixed((128, 256)),
                fixed((128, 256)),
                fixed((1, 256)),
                fixed((1, 128)),
            ],
            out_specs=[by_step(GATE_STEP, 2 * DK)] * 3,
        ),
        compiler_params=params(),
        cost_estimate=cost(2e9, 1e7),
    )(sp, tokens, wsmall, decay_up, gate_up, rate, scale)


def active(mixed, cols, taps):
    count = mixed.shape[0] - 8
    total = taps[0:1] * mixed[5 : 5 + count, cols]
    for j in range(1, CONV):
        total = total + taps[j : j + 1] * mixed[5 + j : 5 + j + count, cols]
    return total * sigmoid(total)


def state_kernel(sp, tokens, halo, log_sums, betas, conv_k, conv_v, *rest):
    parts = rest[:9]
    down_o, solved_o, carry_o, wq_o, state_o, offset_o = rest[9:15]
    halves, wbuf, mixed, state, sems = rest[15:]
    step = pl.program_id(0)

    @pl.when(step == 0)
    def _():
        fetch_weights(sp, parts, halves, wbuf, sems)
        wq_o[...] = wbuf[:, : 2 * DK]
        before = dot(halo[...], wbuf[:, 2 * DK :]).astype(BF).astype(F32)
        mixed[0:8] = before[8:16]
        rr = lax.broadcasted_iota(jnp.int32, (DK, 2 * DK), 0)
        cc = lax.broadcasted_iota(jnp.int32, (DK, 2 * DK), 1)
        start = jnp.where(rr == cc, 1.0, 0.0)
        state[0] = start
        state[1] = start

    mixed[8:] = dot(tokens[...], wbuf[:, 2 * DK :]).astype(BF).astype(F32)
    keys = active(mixed, slice(0, 256), conv_k)
    values = active(mixed, slice(256, 512), conv_v)
    mixed[0:8] = mixed[STATE_STEP : STATE_STEP + 8]

    rows = lax.broadcasted_iota(jnp.int32, (SHARD, SHARD), 0)
    cols = lax.broadcasted_iota(jnp.int32, (SHARD, SHARD), 1)
    places = [
        (h, blk, slice(SHARD * blk, SHARD * blk + SHARD), slice(DK * h, DK * h + DK))
        for blk in range(STATE_STEP // SHARD)
        for h in range(2)
    ]
    systems, sides, ends, tails = [], [], [], []
    for h, blk, ts, hs in places:
        k, beta, log_sum = keys[ts, hs], betas[ts, hs], log_sums[ts, hs]
        k = k * lax.rsqrt(jnp.sum(k * k, axis=1, keepdims=True) + 1e-06)
        end = log_sum[SHARD - 1 : SHARD]
        k_up = k * jnp.exp(log_sum)
        k_down = k * jnp.exp(-log_sum)
        down_o[ts, hs] = k_down
        systems.append(jnp.where(rows > cols, mm3_nt(k_up, k_down), 0.0) * beta)
        sides.append(jnp.concatenate([k_up * beta, values[ts, hs] * beta], axis=1))
        ends.append((k * jnp.exp(end - log_sum)).T)
        tails.append(jnp.where(rows == cols, jnp.exp(end), 0.0))
    inverses = unit_lower_inverses(systems, rows, cols)
    solved = [mm3(t, r) for t, r in zip(inverses, sides)]
    moves = [mm3(e, s) for e, s in zip(ends, solved)]
    for (h, blk, ts, hs), tail, sol, move in zip(places, tails, solved, moves):
        solved_o[ts, 2 * DK * h : 2 * DK * h + 2 * DK] = sol
        carry = state[h]
        carry_o[ts, 2 * DK * h : 2 * DK * h + 2 * DK] = carry
        new = mm3(tail - move[:, :DK], carry)
        state[h, :, :DK] = new[:, :DK]
        state[h, :, DK:] = new[:, DK:] + move[:, DK:]

    @pl.when(step == pl.num_programs(0) - 1)
    def _():
        state_o[...] = state[...]
        offset_o[...] = state[:, :, DK:]


def run_state(sp, tokens, halo, log_sums, betas, conv, parts):
    return pl.pallas_call(
        state_kernel,
        name="block_state",
        out_shape=(
            jax.ShapeDtypeStruct((GROUP, 2 * DK), F32),
            jax.ShapeDtypeStruct((GROUP, 4 * DK), F32),
            jax.ShapeDtypeStruct((GROUP, 4 * DK), F32),
            jax.ShapeDtypeStruct((D, 2 * DK), BF),
            jax.ShapeDtypeStruct((2, DK, 2 * DK), F32),
            jax.ShapeDtypeStruct((2, DK, DK), F32),
        ),
        grid_spec=pltpu.PrefetchScalarGridSpec(
            num_scalar_prefetch=1,
            grid=(GROUP // STATE_STEP,),
            in_specs=[
                by_step(STATE_STEP, D),
                fixed((16, D)),
                by_step(STATE_STEP, 2 * DK),
                by_step(STATE_STEP, 2 * DK),
                columns((CONV, 256), 1),
                columns((CONV, 256), 2),
            ]
            + [pl.BlockSpec(memory_space=pl.ANY)] * 9,
            out_specs=[
                by_step(STATE_STEP, 2 * DK),
                by_step(STATE_STEP, 4 * DK),
                by_step(STATE_STEP, 4 * DK),
                fixed((D, 2 * DK)),
                fixed((2, DK, 2 * DK)),
                fixed((2, DK, DK)),
            ],
            scratch_shapes=[
                pltpu.VMEM((2, NZ, PACK, 128), BF),
                pltpu.VMEM((D, 6 * DK), BF),
                pltpu.VMEM((8 + STATE_STEP, 512), F32),
                pltpu.VMEM((2, DK, 2 * DK), F32),
                pltpu.SemaphoreType.DMA((16,)),
            ],
        ),
        compiler_params=params(),
        cost_estimate=cost(1e10, 2e7),
    )(sp, tokens, halo, log_sums, betas, conv, conv, *parts)


def query_kernel(
    sp, tokens, halo, wq, conv_q, log_sums, k_downs, solved, carries, qeff_o, core_o, mixed
):
    @pl.when(pl.program_id(0) == 0)
    def _():
        before = dot(halo[...], wq[...]).astype(BF).astype(F32)
        mixed[0:8] = before[8:16]

    mixed[8:] = dot(tokens[...], wq[...]).astype(BF).astype(F32)
    query = active(mixed, slice(0, 256), conv_q)
    mixed[0:8] = mixed[QUERY_STEP : QUERY_STEP + 8]
    rows = lax.broadcasted_iota(jnp.int32, (SHARD, SHARD), 0)
    cols = lax.broadcasted_iota(jnp.int32, (SHARD, SHARD), 1)
    places = [
        (
            slice(SHARD * blk, SHARD * blk + SHARD),
            slice(DK * h, DK * h + DK),
            slice(2 * DK * h, 2 * DK * h + 2 * DK),
        )
        for blk in range(QUERY_STEP // SHARD)
        for h in range(2)
    ]
    ups = []
    for ts, hs, _ in places:
        q = query[ts, hs]
        q = q * (lax.rsqrt(jnp.sum(q * q, axis=1, keepdims=True) + 1e-06) * DK**-0.5)
        ups.append(q * jnp.exp(log_sums[ts, hs]))
    scores = [mm3_nt(u, k_downs[ts, hs]) for u, (ts, hs, _) in zip(ups, places)]
    attends = [jnp.where(rows >= cols, a, 0.0) for a in scores]
    withins = [mm3(a, solved[ts, both]) for a, (ts, _, both) in zip(attends, places)]
    outs = [
        mm3(u - w[:, :DK], carries[ts, both]) for u, w, (ts, _, both) in zip(ups, withins, places)
    ]
    for out, w, (ts, hs, _) in zip(outs, withins, places):
        qeff_o[ts, hs] = out[:, :DK]
        core_o[ts, hs] = out[:, DK:] + w[:, DK:]


def run_queries(sp, tokens, halo, wq, conv, log_sums, k_downs, solved, carries):
    wide = jax.ShapeDtypeStruct((GROUP, 2 * DK), F32)
    return pl.pallas_call(
        query_kernel,
        name="block_query",
        out_shape=(wide, wide),
        grid_spec=pltpu.PrefetchScalarGridSpec(
            num_scalar_prefetch=1,
            grid=(GROUP // QUERY_STEP,),
            in_specs=[
                by_step(QUERY_STEP, D),
                fixed((16, D)),
                fixed((D, 2 * DK)),
                columns((CONV, 256), 0),
                by_step(QUERY_STEP, 2 * DK),
                by_step(QUERY_STEP, 2 * DK),
                by_step(QUERY_STEP, 4 * DK),
                by_step(QUERY_STEP, 4 * DK),
            ],
            out_specs=[by_step(QUERY_STEP, 2 * DK)] * 2,
            scratch_shapes=[pltpu.VMEM((8 + QUERY_STEP, 256), F32)],
        ),
        compiler_params=params(),
        cost_estimate=cost(5e9, 2e7),
    )(sp, tokens, halo, wq, conv, log_sums, k_downs, solved, carries)


def finish_kernel(near, middle, far, qeff, core, gate, gain, out, state):
    heads = range(2)

    @pl.when(pl.program_id(0) == 0)
    def _():
        carries = [middle[h, :, DK:] + mm3(middle[h, :, :DK], far[h]) for h in heads]
        starts = [near[h, :, DK:] + mm3(near[h, :, :DK], carries[h]) for h in heads]
        for h in heads:
            state[h] = starts[h]

    spans = [slice(DK * h, DK * h + DK) for h in heads]
    added = [mm3(qeff[:, hs], state[h]) for h, hs in zip(heads, spans)]
    for hs, more in zip(spans, added):
        full = core[:, hs] + more
        scale = lax.rsqrt(jnp.mean(full * full, axis=1, keepdims=True) + 1e-06)
        out[:, hs] = (full * scale * gain[...] * gate[:, hs]).astype(BF)


def run_finish(near, middle, far, qeff, core, gate, gain):
    def whole(shape):
        return pl.BlockSpec(shape, lambda i: (0,) * len(shape))

    tile = pl.BlockSpec((512, 2 * DK), lambda i: (i, 0))
    return pl.pallas_call(
        finish_kernel,
        name="finish",
        out_shape=jax.ShapeDtypeStruct((GROUP, 2 * DK), BF),
        grid=(GROUP // 512,),
        in_specs=[
            whole((2, DK, 2 * DK)),
            whole((2, DK, 2 * DK)),
            whole((2, DK, DK)),
            tile,
            tile,
            tile,
            whole((1, DK)),
        ],
        out_specs=tile,
        scratch_shapes=[pltpu.VMEM((2, DK, DK), F32)],
        compiler_params=pltpu.CompilerParams(vmem_limit_bytes=VMEM_LIMIT),
    )(near, middle, far, qeff, core, gate, gain)


def gather_weights(weight, c, y):
    rows = lax.dynamic_slice(weight, (ROWS * lax.rem(y, 2), 0), (ROWS, 3 * UNIT))
    whole = jnp.where(c == 0, rows[:, : 2 * UNIT], rows[:, UNIT:])
    half = jnp.where(c == 0, rows[:, 2 * UNIT :], rows[:, :UNIT])
    half = jnp.concatenate([half[:PACK], half[PACK:]], axis=1)
    seq = ("z", "x", "c")
    mine = jnp.concatenate(
        [lax.ppermute(whole, seq, WHOLE_ROUTE), lax.ppermute(half, seq, HALF_ROUTE)], axis=0
    )
    near = [mine] + [lax.ppermute(mine, "z", ring(k)) for k in range(1, NZ)]
    far = [lax.ppermute(p, "y", ring(d)) for p, d in zip(near, (1, 3, 1, 3)) if p is not near[1]]
    last = [lax.ppermute(p, "y", ring(d)) for p, d in ((near[1][:ROWS], 3), (near[1][ROWS:], 1))]
    return near, far[:1] + last[:1] + far[1:] + last[1:]


def per_device(
    tokens,
    qkv_weight,
    conv_weight,
    decay_down,
    decay_up,
    decay_rate,
    beta_weight,
    beta_scale,
    gate_down,
    gate_up,
    norm_gain,
):
    z, x, c, y = (lax.axis_index(a) for a in ("z", "x", "c", "y"))
    g = x * NC + c
    wsmall = jnp.concatenate(
        [decay_down, gate_down, jnp.pad(beta_weight, ((0, 0), (0, 128 - H)))], axis=1
    )
    head = first_head(x, c)
    sp = jnp.concatenate([jnp.stack([z, y, head]).astype(jnp.int32), jnp.asarray(TABLES)[g]])

    def mine(array, start=0):
        return jnp.concatenate(
            [
                lax.dynamic_slice(array, (0, start + DK * (head + 4 * h)), (array.shape[0], DK))
                for h in range(2)
            ],
            axis=1,
        )

    taps = jnp.concatenate([mine(conv_weight, HV * kind) for kind in range(3)], axis=1)
    scale = jnp.pad(beta_scale, (0, 128 - H)).reshape(1, 128)
    row = lax.all_gather(tokens, ("x", "c"), axis=0, tiled=True)
    near, far = gather_weights(qkv_weight, c, y)
    halo = lax.ppermute(row[GROUP - 16 :], "z", ahead(1))
    log_sums, betas, gate = run_gates(
        sp,
        row,
        wsmall,
        mine(decay_up),
        mine(gate_up),
        mine(decay_rate.reshape(1, HV)),
        scale,
    )
    k_downs, solved, carries, wq, state, offset = run_state(
        sp, row, halo, log_sums, betas, taps, near + far
    )
    first = lax.ppermute(state, "z", ahead(1))
    second = lax.ppermute(state, "z", ahead(2))
    third = lax.ppermute(offset, "z", ahead(3))
    qeff, core = run_queries(sp, row, halo, wq, taps, log_sums, k_downs, solved, carries)
    out = run_finish(first, second, third, qeff, core, gate, norm_gain.reshape(1, DK))
    out = lax.all_to_all(out.reshape(ROW, SHARD, 2 * DK), ("x", "c"), 0, 0)
    heads = {
        first_head(i // NC, i % NC) + 4 * h: out[i, :, DK * h : DK * h + DK]
        for i in range(ROW)
        for h in range(2)
    }
    return jnp.concatenate([heads[h] for h in range(H)], axis=1)


def solution(mesh):
    fine = Mesh(mesh.devices.reshape(NZ, NX, NC, NY), ("z", "x", "c", "y"))
    seq = ("z", "x", "c")
    in_specs = (P(("y",) + seq, None), P(None, seq)) + (P(),) * 9
    return jax.shard_map(
        per_device,
        mesh=fine,
        in_specs=in_specs,
        out_specs=P(("y",) + seq, None),
        check_vma=False,
    )
```
